256 devices in a mesh: lat: 8 (over x_hi, y), lon: 32 (over x_lo, z, core).
Axes of the slice: x: 4 (x_hi: 2, x_lo: 2; x = x_hi * 2 + x_lo), y: 4, z: 8, core: 2. Of those that a mesh axis runs over, the one named last changes fastest.
Arguments:
- sea_state: bfloat16 [64, 256, 4096], P(None, 'lat', 'lon'), may hold values from -60 to 60
- conv_kernel: bfloat16 [64, 49], replicated, may hold values from -0.875 to 0.875
- conv_bias: bfloat16 [64], replicated, may hold values from -3 to 3
- norm_gain: bfloat16 [64], replicated, may hold values from 0.25 to 1.75
- norm_shift: bfloat16 [64], replicated, may hold values from -3 to 3
- w_in: bfloat16 [64, 256], replicated, may hold values from -0.75 to 0.75
- b_in: bfloat16 [256], replicated, may hold values from -3 to 3
- w_out: bfloat16 [256, 64], replicated, may hold values from -0.375 to 0.375
- b_out: bfloat16 [64], replicated, may hold values from -3 to 3
- layer_scale: bfloat16 [64], replicated, may hold values from 0.29882812 to 1
- sea_mask: int32 [256, 4096], P('lat', 'lon'), may hold values 0 or 1
- cotangent: bfloat16 [64, 256, 4096], P(None, 'lat', 'lon'), may hold values from -6 to 6
Outputs:
- new_state: bfloat16 [64, 256, 4096], P(None, 'lat', 'lon')
- state_grad: bfloat16 [64, 256, 4096], P(None, 'lat', 'lon')
- kernel_grad: float32 [64, 49], replicated
- w_in_grad: float32 [64, 256], replicated
- w_out_grad: float32 [256, 64], replicated
- b_in_grad: float32 [256], replicated
- channel_grads: float32 [5, 64], replicated
The draws below stay inside these ranges and needn't reach their ends.
Inputs may be any that keep to these rules, and one draw needn't show every extreme that they name: `sea_mask`: 1 marks an ocean cell, 0 land.
All inputs are finite; a program needn't handle non-finite values. No bound on the sum of `sea_mask` on one device may be relied on, other than what follows from the above.
Results may differ from the reference program's by a relative error of at most 0.0062.
Values sent between devices are 32-bit elements; how exact they have to be, the bound alone decides.
No kernel may reach another device: no remote copies, remote signals or barrier semaphores. Data moves between devices by JAX's collectives and lax.ppermute only.
A program may use at most 128 MiB of HBM per device.

```python
import math
import jax
import jax.numpy as jnp
from jax import lax

C = 64
HID = 256
NLAT = 256
NLON = 4096


def draw_sea_state(key, part):
    key_base, key_rows, key_cols = jax.random.split(key, 3)
    base_field = jnp.clip(jax.random.normal(key_base, (C, NLAT, NLON), jnp.float32), -6.0, 6.0)
    half_range = 0.5 * math.log(10.0)
    row_factor = jnp.exp(jax.random.uniform(key_rows, (1, NLAT, 1), jnp.float32, 0.0, half_range))
    col_factor = jnp.exp(jax.random.uniform(key_cols, (1, 1, NLON), jnp.float32, 0.0, half_range))
    return (base_field * row_factor * col_factor).astype(jnp.bfloat16)


def set_ends(values, key, low, top_value):
    longest = values.shape.index(max(values.shape))
    spots = []
    for shift in (0, 1):
        where = [jax.random.randint(jax.random.fold_in(key, axis), (), 0, length) for axis, length in enumerate(values.shape)]
        where[longest] = (where[longest] + shift) % values.shape[longest]
        spots.append(tuple(where))
    return values.at[spots[0]].set(low).at[spots[1]].set(top_value)


def steps_of(rng, dims, pieces, low, largest):
    level = 1.0
    for axis_at, shards_of in pieces:
        heights = jax.random.uniform(jax.random.fold_in(jax.random.fold_in(rng, 6), axis_at), (shards_of,), jnp.float32, low / len(pieces), largest / len(pieces))
        level = level * jnp.repeat(jnp.exp(heights), dims[axis_at] // shards_of).reshape((-1,) + (1,) * (len(dims) - 1 - axis_at))
    return level


def bell_draw(stream_key, shape, scale, most, cuts=(), kind=jnp.bfloat16):
    gain = steps_of(stream_key, shape, cuts, -0.22, 0.18) if cuts else 1.0
    result = jax.random.normal(stream_key, shape, jnp.float32) * scale * gain
    return jnp.minimum(jnp.maximum(result, -most), most).astype(kind)


def setup_inputs(seed: int = 0) -> dict:
    splits = jax.random.split(jax.random.key(seed), 13)
    sea_state = draw_sea_state(jax.random.fold_in(splits[12], 71), 0)
    conv_kernel = bell_draw(splits[1], (C, 49), 49 ** -0.5, 0.875)
    conv_bias = bell_draw(splits[2], (C,), 0.5, 3.0)
    norm_gain = jnp.clip(1.0 + 0.15 * jax.random.normal(splits[3], (C,), jnp.float32), 0.25, 1.75).astype(jnp.bfloat16)
    norm_shift = bell_draw(splits[4], (C,), 0.5, 3.0)
    w_in = bell_draw(splits[5], (C, HID), C ** -0.5, 0.75)
    b_in = bell_draw(splits[6], (HID,), 0.5, 3.0)
    w_out = bell_draw(splits[7], (HID, C), HID ** -0.5, 0.375)
    b_out = bell_draw(splits[8], (C,), 0.5, 3.0)
    layer_scale = jnp.clip(jax.random.uniform(splits[9], (C,), jnp.float32, 0.29882812, 1.0), 0.29882812, 1.0).astype(jnp.bfloat16)
    sea_mask = set_ends((jax.random.randint(splits[10], (NLAT, NLON), 0, 4) < 3).astype(jnp.int32), jax.random.fold_in(splits[10], 1), 0, 1)
    cotangent = bell_draw(splits[11], (C, NLAT, NLON), 1.0, 6.0, ((1, 8), (2, 32)))
    return {"sea_state": sea_state, "conv_kernel": conv_kernel, "conv_bias": conv_bias, "norm_gain": norm_gain, "norm_shift": norm_shift, "w_in": w_in, "b_in": b_in, "w_out": w_out, "b_out": b_out, "layer_scale": layer_scale, "sea_mask": sea_mask, "cotangent": cotangent}


slope_coef = 0.044715
tanh_scale = math.sqrt(2.0 / math.pi)
ln_epsilon = 1e-06

def depthwise(padded, conv_kernel, conv_bias, row_count, col_count):
    weights = conv_kernel.astype(jnp.float32)
    running = jnp.zeros((padded.shape[0], row_count, col_count), jnp.float32) + conv_bias.astype(jnp.float32)[:, None, None]
    for row_off in range(7):
        for col_off in range(7):
            window = padded[:, row_off:row_off + row_count, col_off:col_off + col_count].astype(jnp.float32)
            running = running + weights[:, 7 * row_off + col_off][:, None, None] * window
    return running

def kernel_grads(padded, conv_grad):
    row_count = conv_grad.shape[1]
    col_count = conv_grad.shape[2]
    columns = []
    for row_off in range(7):
        for col_off in range(7):
            window = padded[:, row_off:row_off + row_count, col_off:col_off + col_count].astype(jnp.float32)
            columns.append(lax.optimization_barrier(jnp.sum(conv_grad * window, axis=(1, 2))))
    return jnp.stack(columns, axis=1)

def spread_back(conv_grad, conv_kernel):
    row_count = conv_grad.shape[1]
    col_count = conv_grad.shape[2]
    weights = conv_kernel.astype(jnp.float32)
    widened = jnp.pad(conv_grad, ((0, 0), (6, 6), (6, 6)))
    running = jnp.zeros((conv_grad.shape[0], row_count + 6, col_count + 6), jnp.float32)
    for row_off in range(7):
        for col_off in range(7):
            window = widened[:, 6 - row_off:12 - row_off + row_count, 6 - col_off:12 - col_off + col_count]
            running = running + weights[:, 7 * row_off + col_off][:, None, None] * window
    return running

def pointwise(conv_out, sea_state, cotangent, sea_mask, norm_gain, norm_shift, w_in, b_in, w_out, b_out, layer_scale):
    chan_count = conv_out.shape[0]
    flat_conv = conv_out.reshape(chan_count, -1)
    centre = flat_conv - lax.optimization_barrier(jnp.mean(flat_conv, axis=0, keepdims=True))
    inv_std = lax.rsqrt(lax.optimization_barrier(jnp.mean(centre * centre, axis=0, keepdims=True)) + ln_epsilon)
    unit_norm = centre * inv_std
    gain_col = norm_gain.astype(jnp.float32)[:, None]
    normed = (unit_norm * gain_col + norm_shift.astype(jnp.float32)[:, None]).astype(jnp.bfloat16)
    pre_act = jnp.dot(w_in.T, normed, preferred_element_type=jnp.float32) + b_in.astype(jnp.float32)[:, None]
    tangent = jnp.tanh(tanh_scale * (pre_act + slope_coef * pre_act * pre_act * pre_act))
    hidden = (0.5 * pre_act * (1.0 + tangent)).astype(jnp.bfloat16)
    mixed_out = jnp.dot(w_out.T, hidden, preferred_element_type=jnp.float32) + b_out.astype(jnp.float32)[:, None]
    ocean_mask = sea_mask.reshape(1, -1).astype(jnp.float32)
    scale_col = layer_scale.astype(jnp.float32)[:, None]
    state_flat = sea_state.reshape(chan_count, -1).astype(jnp.float32)
    new_state = (ocean_mask * (state_flat + scale_col * mixed_out)).astype(jnp.bfloat16)
    masked_cot = ocean_mask * cotangent.reshape(chan_count, -1).astype(jnp.float32)
    mixed_grad = (scale_col * masked_cot).astype(jnp.bfloat16)
    scale_sum = lax.optimization_barrier(jnp.sum(masked_cot * mixed_out, axis=1))
    out_bias_sum = lax.optimization_barrier(jnp.sum(mixed_grad.astype(jnp.float32), axis=1))
    cell_axes = (((1,), (1,)), ((), ()))
    out_weight_sum = lax.dot_general(hidden, mixed_grad, cell_axes, preferred_element_type=jnp.float32)
    hidden_grad = jnp.dot(w_out, mixed_grad, preferred_element_type=jnp.float32)
    gelu_slope = 0.5 * (1.0 + tangent) + 0.5 * pre_act * (1.0 - tangent * tangent) * tanh_scale * (1.0 + 3.0 * slope_coef * pre_act * pre_act)
    pre_grad = (hidden_grad * gelu_slope).astype(jnp.bfloat16)
    in_bias_sum = lax.optimization_barrier(jnp.sum(pre_grad.astype(jnp.float32), axis=1))
    in_weight_sum = lax.dot_general(normed, pre_grad, cell_axes, preferred_element_type=jnp.float32)
    normed_grad = jnp.dot(w_in, pre_grad, preferred_element_type=jnp.float32)
    gain_sum = lax.optimization_barrier(jnp.sum(normed_grad * unit_norm, axis=1))
    shift_sum = lax.optimization_barrier(jnp.sum(normed_grad, axis=1))
    unit_grad = normed_grad * gain_col
    conv_grad = inv_std * (unit_grad - lax.optimization_barrier(jnp.mean(unit_grad, axis=0, keepdims=True)) - unit_norm * lax.optimization_barrier(jnp.mean(unit_grad * unit_norm, axis=0, keepdims=True)))
    partial_sums = (scale_sum, out_bias_sum, out_weight_sum, in_bias_sum, in_weight_sum, gain_sum, shift_sum)
    return (new_state.reshape(conv_out.shape), conv_grad.reshape(conv_out.shape), masked_cot.reshape(conv_out.shape), partial_sums)

def reference(sea_state, conv_kernel, conv_bias, norm_gain, norm_shift, w_in, b_in, w_out, b_out, layer_scale, sea_mask, cotangent):
    chan_count = sea_state.shape[0]
    wrapped = jnp.concatenate([sea_state[:, :, NLON - 3:], sea_state, sea_state[:, :, :3]], axis=2)
    ghost_rows = wrapped[:, NLAT - 3:, ::-1][:, ::-1, :]
    padded = jnp.concatenate([jnp.zeros((chan_count, 3, NLON + 6), sea_state.dtype), wrapped, ghost_rows], axis=1)
    conv_out = depthwise(padded, conv_kernel, conv_bias, NLAT, NLON)
    block_count = NLAT // 8

    def to_blocks(array):
        return jnp.moveaxis(array.reshape(array.shape[0], block_count, 8, NLON), 1, 0)

    def block_step(running, block_data):
        conv_piece, state_piece, cot_piece, mask_piece = block_data
        new_piece, grad_piece, masked_piece, partial_sums = pointwise(conv_piece, state_piece, cot_piece, mask_piece, norm_gain, norm_shift, w_in, b_in, w_out, b_out, layer_scale)
        return (tuple((left + right for left, right in zip(running, partial_sums))), (new_piece, grad_piece))
    zero_init = (jnp.zeros((chan_count,), jnp.float32), jnp.zeros((chan_count,), jnp.float32), jnp.zeros((HID, chan_count), jnp.float32), jnp.zeros((HID,), jnp.float32), jnp.zeros((chan_count, HID), jnp.float32), jnp.zeros((chan_count,), jnp.float32), jnp.zeros((chan_count,), jnp.float32))
    totals, (new_blocks, grad_blocks) = lax.scan(block_step, zero_init, (to_blocks(conv_out), to_blocks(sea_state), to_blocks(cotangent), sea_mask.reshape(block_count, 8, NLON)))
    scale_sum, out_bias_sum, out_weight_sum, in_bias_sum, in_weight_sum, gain_sum, shift_sum = totals
    new_state = jnp.moveaxis(new_blocks, 0, 1).reshape(chan_count, NLAT, NLON)
    conv_grad = jnp.moveaxis(grad_blocks, 0, 1).reshape(chan_count, NLAT, NLON)
    spread = spread_back(conv_grad, conv_kernel)
    col_fold = spread[:, :, 3:NLON + 3]
    col_fold = col_fold.at[:, :, NLON - 3:].add(spread[:, :, :3])
    col_fold = col_fold.at[:, :, :3].add(spread[:, :, NLON + 3:])
    row_fold = col_fold[:, 3:NLAT + 3]
    row_fold = row_fold.at[:, NLAT - 3:].add(col_fold[:, NLAT + 3:, ::-1][:, ::-1, :])
    direct = sea_mask.astype(jnp.float32)[None] * cotangent.astype(jnp.float32)
    state_grad = (direct + row_fold).astype(jnp.bfloat16)
    grad_scale = 1.0 / math.sqrt(NLAT * NLON)
    kernel_grad = grad_scale * kernel_grads(padded, conv_grad)
    channel_grads = grad_scale * jnp.stack([lax.optimization_barrier(jnp.sum(conv_grad, axis=(1, 2))), gain_sum, shift_sum, out_bias_sum, scale_sum])
    return (new_state, state_grad, kernel_grad, grad_scale * in_weight_sum, grad_scale * out_weight_sum, grad_scale * in_bias_sum, channel_grads)
```

```python
import functools
import math

import jax
import jax.numpy as jnp
from jax import lax
from jax.experimental import pallas as pl
from jax.experimental.pallas import tpu as pltpu
from jax.sharding import PartitionSpec as P

slope_coef = 0.044715
tanh_scale = math.sqrt(2.0 / math.pi)
ln_epsilon = 1e-06
f32, bf16 = jnp.float32, jnp.bfloat16

CH, ROWS, COLS, HID = 64, 32, 128, 256
PAD = ROWS + 6
AXES = ("lat", "lon")
VM = pl.BlockSpec(memory_space=pltpu.VMEM)
SM = pl.BlockSpec(memory_space=pltpu.SMEM)
VMEM_LIMIT = 60 * 1024 * 1024


def call(body, out_shape, args, scratch=(), smem_first=False, flops=0, nbytes=0, name=None):
    specs = [VM] * len(args)
    if smem_first:
        specs[0] = SM
    return pl.pallas_call(
        body,
        out_shape=out_shape,
        in_specs=specs,
        out_specs=jax.tree.map(lambda _: VM, out_shape),
        scratch_shapes=list(scratch),
        compiler_params=pltpu.CompilerParams(vmem_limit_bytes=VMEM_LIMIT),
        cost_estimate=pl.CostEstimate(flops=flops, bytes_accessed=nbytes, transcendentals=0),
        name=name,
    )(*args)


def lanes():
    return lax.broadcasted_iota(jnp.int32, (CH, COLS), 1)


def to_rows(src, tall, put):
    def fill(c, carry):
        part = src[pl.ds(c * 8, 8)].astype(f32)
        tall[pl.ds(pl.multiple_of(c * 8 * ROWS, 8 * ROWS), 8 * ROWS), :] = part.reshape(8 * ROWS, COLS)
        return carry

    lax.fori_loop(0, CH // 8, fill, 0)

    def take(r, carry):
        put(r, tall[pl.ds(r, CH, stride=ROWS), :])
        return carry

    lax.fori_loop(0, ROWS, take, 0)


def from_rows(tall, dst):
    def drain(c, carry):
        part = tall[pl.ds(pl.multiple_of(c * 8 * ROWS, 8 * ROWS), 8 * ROWS), :]
        dst[pl.ds(c * 8, 8)] = part.reshape(8, ROWS, COLS).astype(bf16)
        return carry

    lax.fori_loop(0, CH // 8, drain, 0)


def prepare_body(state, cot, mask, state_rows, cot_rows, tall, tall2):
    def put_state(r, value):
        state_rows[r] = value

    def put_cot(r, value):
        cot_rows[r] = value * mask[pl.ds(r, 1), :]

    to_rows(state, tall, put_state)
    to_rows(cot, tall2, put_cot)


def edges_body(flags, from_a, from_b, rows, north, south, to_west, to_east):
    even = flags[0] == 1
    on_top = flags[1] == 1
    for g in range(3):
        south[g] = jnp.where(even, from_b[g], from_a[g])

    @pl.when(jnp.logical_not(on_top))
    def _():
        for g in range(3):
            north[g] = jnp.where(even, from_a[g], from_b[g])

    @pl.when(on_top)
    def _():
        back = COLS - 1 - lanes()
        for g in range(3):
            got = jnp.where(even, from_a[2 - g], from_b[2 - g])
            north[g] = jnp.take_along_axis(got, back, axis=1)

    lane = lanes()

    def pack(spot, value, carry):
        west, east = carry
        here = jnp.logical_and(lane >= 3 * spot, lane < 3 * spot + 3)
        west = jnp.where(here, pltpu.roll(value, 3 * spot, 1), west)
        east = jnp.where(here, pltpu.roll(value, 3 * spot + 3, 1), east)
        return west, east

    carry = (jnp.zeros((CH, COLS), f32), jnp.zeros((CH, COLS), f32))
    for g in range(3):
        carry = pack(g, south[g], carry)
        carry = pack(g + 3 + ROWS, north[g], carry)
    carry = lax.fori_loop(0, ROWS, lambda r, c: pack(r + 3, rows[r], c), carry)
    to_west[...], to_east[...] = carry


def shift_row(shifted, spot, value, west, east, lane):
    west_here = pltpu.roll(west[...], 125 - 3 * spot, 1)
    east_here = pltpu.roll(east[...], lax.rem(COLS - 3 * spot, COLS), 1)
    for b in range(7):
        off = b - 3
        if off == 0:
            shifted[b, spot] = value
        elif off < 0:
            shifted[b, spot] = pltpu.roll(jnp.where(lane >= COLS + off, west_here, value), -off, 1)
        else:
            shifted[b, spot] = pltpu.roll(jnp.where(lane < off, east_here, value), COLS - off, 1)


def shift_all(shifted, rows, south, north, west, east):
    lane = lanes()

    def low(g, carry):
        shift_row(shifted, g, south[g], west, east, lane)
        shift_row(shifted, g + 3 + ROWS, north[g], west, east, lane)
        return carry

    def mid(r, carry):
        shift_row(shifted, r + 3, rows[r], west, east, lane)
        return carry

    lax.fori_loop(0, 3, low, 0)
    lax.fori_loop(0, ROWS, mid, 0)


def taps(shifted, weights, r0, c0, acc, flip):
    rows = acc.shape[0]
    for b in range(7):
        window = shifted[b, pl.ds(r0, rows + 6), pl.ds(c0, 8), :]
        for a in range(7):
            t = 7 * a + b
            t = 48 - t if flip else t
            acc = acc + weights[t, pl.ds(c0, 8), :][None] * window[a : a + rows]
    return acc


def main_body(
    state_rows,
    south,
    north,
    west,
    east,
    cot_rows,
    mask,
    weights,
    chan,
    b_in,
    w_in,
    w_in_t,
    w_out,
    w_out_t,
    new_rows,
    conv_grad,
    sums,
    shifted,
    conv_out,
    win_acc,
    wout_acc,
    bin_acc,
    gain_acc,
    shift_acc,
    obias_acc,
    scale_acc,
):
    shift_all(shifted, state_rows, south, north, west, east)

    def conv_step(i, carry):
        c0 = pl.multiple_of((i // 4) * 8, 8)
        r0 = (i % 4) * 8
        bias = chan[0, pl.ds(c0, 8), :]
        acc = jnp.broadcast_to(bias[None], (8, 8, COLS))
        conv_out[pl.ds(r0, 8), pl.ds(c0, 8), :] = taps(shifted, weights, r0, c0, acc, False)
        return carry

    lax.fori_loop(0, 32, conv_step, 0)

    for acc in (win_acc, wout_acc, bin_acc, gain_acc, shift_acc, obias_acc, scale_acc):
        acc[...] = jnp.zeros_like(acc)

    def wide(x):
        return jnp.concatenate([x, x], axis=1)

    def fold(x):
        return x[:, :COLS] + x[:, COLS:]

    def mean(x):
        return jnp.sum(x, axis=0, keepdims=True) * (1.0 / CH)

    cells = (((1,), (1,)), ((), ()))

    def point_step(g, carry):
        r = 2 * g
        gain, shift, out_bias, scale = (wide(chan[k]) for k in range(1, 5))
        x = jnp.concatenate([conv_out[r], conv_out[r + 1]], axis=1)
        centre = x - mean(x)
        inv_std = lax.rsqrt(mean(centre * centre) + ln_epsilon)
        unit = centre * inv_std
        normed = (unit * gain + shift).astype(bf16)
        masked_cot = jnp.concatenate([cot_rows[r], cot_rows[r + 1]], axis=1)
        mixed_grad = (scale * masked_cot).astype(bf16)
        u = jnp.dot(w_in_t[...], normed, preferred_element_type=f32) + wide(b_in[...])
        hidden_grad = jnp.dot(w_out[...], mixed_grad, preferred_element_type=f32)
        u2 = u * u
        t = jnp.tanh(u * (tanh_scale + (tanh_scale * slope_coef) * u2))
        half = 0.5 * u
        hidden = (half + half * t).astype(bf16)
        slope = 0.5 + 0.5 * t + half * (1.0 - t * t) * (
            tanh_scale + (3.0 * tanh_scale * slope_coef) * u2
        )
        pre_grad = (hidden_grad * slope).astype(bf16)
        bin_acc[...] += fold(pre_grad.astype(f32))
        mixed = jnp.dot(w_out_t[...], hidden, preferred_element_type=f32) + out_bias
        normed_grad = jnp.dot(w_in[...], pre_grad, preferred_element_type=f32)
        win_acc[...] += lax.dot_general(normed, pre_grad, cells, preferred_element_type=f32)
        wout_acc[...] += lax.dot_general(hidden, mixed_grad, cells, preferred_element_type=f32)
        state = jnp.concatenate([state_rows[r], state_rows[r + 1]], axis=1)
        ocean = jnp.concatenate([mask[pl.ds(r, 1), :], mask[pl.ds(r + 1, 1), :]], axis=1)
        new = ocean * (state + scale * mixed)
        new_rows[r] = new[:, :COLS]
        new_rows[r + 1] = new[:, COLS:]
        scale_acc[...] += fold(masked_cot * mixed)
        obias_acc[...] += fold(mixed_grad.astype(f32))
        gain_acc[...] += fold(normed_grad * unit)
        shift_acc[...] += fold(normed_grad)
        q = normed_grad * gain
        grad = inv_std * (q - mean(q) - unit * mean(q * unit))
        conv_grad[r] = grad[:, :COLS]
        conv_grad[r + 1] = grad[:, COLS:]
        return carry

    lax.fori_loop(0, ROWS // 2, point_step, 0)

    lane8 = lax.broadcasted_iota(jnp.int32, (8, COLS), 1)

    def total(x):
        return jnp.broadcast_to(jnp.sum(x, axis=1, keepdims=True), (8, COLS))

    def kernel_step(i, carry):
        c0 = pl.multiple_of(i * 8, 8)
        out = jnp.zeros((8, COLS), f32)
        bias = conv_grad[0, pl.ds(c0, 8), :]
        for r in range(1, ROWS):
            bias = bias + conv_grad[r, pl.ds(c0, 8), :]
        small = (
            bias,
            gain_acc[pl.ds(c0, 8), :],
            shift_acc[pl.ds(c0, 8), :],
            obias_acc[pl.ds(c0, 8), :],
            scale_acc[pl.ds(c0, 8), :],
        ) + tuple(bin_acc[pl.ds(CH * k + c0, 8), :] for k in range(4))
        for k, x in enumerate(small):
            out = jnp.where(lane8 == 49 + k, total(x), out)

        def column(b, out):
            window = [shifted[b, a, pl.ds(c0, 8), :] for a in range(7)]
            acc = None
            for r in range(ROWS):
                grad = conv_grad[r, pl.ds(c0, 8), :]
                terms = [grad * w for w in window]
                acc = terms if acc is None else [p + q for p, q in zip(acc, terms)]
                if r + 1 < ROWS:
                    window = window[1:] + [shifted[b, r + 7, pl.ds(c0, 8), :]]
            for a in range(7):
                out = jnp.where(lane8 == 7 * a + b, total(acc[a]), out)
            return out

        out = lax.fori_loop(0, 7, column, out)
        sums[pl.ds(pl.multiple_of(256 + c0, 8), 8), :] = out
        return carry

    lax.fori_loop(0, CH // 8, kernel_step, 0)
    sums[0:64, :] = win_acc[:, :COLS]
    sums[64:128, :] = win_acc[:, COLS:]
    sums[128:256, :] = jnp.concatenate([wout_acc[0:128, :], wout_acc[128:256, :]], axis=1)


def spread_body(
    flags,
    conv_grad,
    south,
    north,
    west,
    east,
    weights,
    cot_rows,
    new_rows,
    state_grad,
    new_state,
    shifted,
    tall,
):
    def put_new(r, carry):
        tall[pl.ds(r, CH, stride=ROWS), :] = new_rows[r]
        return carry

    lax.fori_loop(0, ROWS, put_new, 0)
    from_rows(tall, new_state)

    shift_all(shifted, conv_grad, south, north, west, east)
    on_top = flags[1] == 1

    def spread_step(i, carry):
        c0 = pl.multiple_of((i // 3) * 8, 8)
        r0 = (i % 3) * 8
        acc = cot_rows[pl.ds(r0, 8), pl.ds(c0, 8), :]
        acc = taps(shifted, weights, r0, c0, acc, True)
        for k in range(8):
            tall[pl.ds(c0 * ROWS + r0 + k, 8, stride=ROWS), :] = acc[k]
        return carry

    lax.fori_loop(0, 24, spread_step, 0)

    def top_step(i, carry):
        c0 = pl.multiple_of(i * 8, 8)
        acc = [cot_rows[24 + k, pl.ds(c0, 8), :] for k in range(8)]
        for b in range(7):
            for p in range(14):
                value = shifted[b, 24 + p, pl.ds(c0, 8), :]
                for k in range(8):
                    a = p - k
                    if not 0 <= a < 7:
                        continue
                    t = 7 * a + b
                    if p < 11:
                        w = weights[48 - t, pl.ds(c0, 8), :]
                    else:
                        w = weights[jnp.where(on_top, t, 48 - t), pl.ds(c0, 8), :]
                    acc[k] = acc[k] + w * value
        for k in range(8):
            tall[pl.ds(c0 * ROWS + 24 + k, 8, stride=ROWS), :] = acc[k]
        return carry

    lax.fori_loop(0, CH // 8, top_step, 0)
    from_rows(tall, state_grad)


def unpack_body(sums, kernel_grad, w_in_grad, w_out_grad, b_in_grad, channel_grads, *, scale):
    w_in_grad[:, :COLS] = sums[0:64, :] * scale
    w_in_grad[:, COLS:] = sums[64:128, :] * scale
    packed = sums[128:256, :] * scale
    w_out_grad[0:128, :] = packed[:, :CH]
    w_out_grad[128:256, :] = packed[:, CH:]
    tail = sums[256:320, :] * scale
    kernel_grad[...] = tail[:, :49]
    turned = jnp.transpose(jnp.concatenate([tail, tail], axis=0))
    channel_grads[...] = turned[49:54, :CH]
    for k in range(4):
        b_in_grad[:, CH * k : CH * k + CH] = turned[54 + k : 55 + k, :CH]


def row_pairs(lat_size, lon_size):
    first, second = [], []
    for i in range(lat_size):
        for j in range(lon_size):
            me = i * lon_size + j
            first.append((me, (i ^ 1) * lon_size + j))
            if i == lat_size - 1:
                second.append((me, i * lon_size + lon_size - 1 - j))
            elif i > 0:
                other = i + 1 if i % 2 else i - 1
                second.append((me, other * lon_size + j))
    return first, second


def exchange_rows(flags, top, bottom):
    first, second = row_pairs(lax.axis_size("lat"), lax.axis_size("lon"))
    even = flags[0] == 1
    from_a = lax.ppermute(jnp.where(even, top, bottom), AXES, first)
    from_b = lax.ppermute(jnp.where(even, bottom, top), AXES, second)
    return from_a, from_b


def settle_edges(flags, from_a, from_b, rows):
    slab = jax.ShapeDtypeStruct((3, CH, COLS), f32)
    flat = jax.ShapeDtypeStruct((CH, COLS), f32)
    return call(
        edges_body,
        (slab, slab, flat, flat),
        (flags, from_a, from_b, rows),
        smem_first=True,
        flops=1 << 20,
        nbytes=1 << 21,
        name="edges",
    )


def exchange_columns(to_west, to_east):
    lon_size = lax.axis_size("lon")
    up = [(j, (j + 1) % lon_size) for j in range(lon_size)]
    down = [(k, j) for j, k in up]
    west = lax.ppermute(to_east, "lon", up)
    east = lax.ppermute(to_west, "lon", down)
    return west, east


def core_pairs():
    return [(i, i ^ 1) for i in range(32)]


def lat_pairs(flip_y, flip_x):
    return [(i, ((i >> 2) ^ flip_x) * 4 + ((i & 3) ^ flip_y)) for i in range(8)]


def reduce_and_spread(sums, flags, conv_grad, finish):
    odd = lax.rem(lax.axis_index("lon"), 2) == 1
    half = sums.shape[0] // 2
    low, high = sums[:half], sums[half:]
    mine = jnp.where(odd, high, low) + lax.ppermute(jnp.where(odd, low, high), "lon", core_pairs())
    groups = [[2 * k + core for k in range(16)] for core in range(2)]
    piece = half // 16

    def swap(x):
        return lax.all_to_all(x, "lon", 0, 0, tiled=True, axis_index_groups=groups)

    from_a, from_b = exchange_rows(flags, conv_grad[ROWS - 3 :], conv_grad[:3])
    got = swap(mine.reshape(16, piece, COLS))
    north, south, to_west, to_east = settle_edges(flags, from_a, from_b, conv_grad)
    got, to_west, to_east = lax.optimization_barrier((got, to_west, to_east))
    part = jnp.sum(got, axis=0)
    west, east = exchange_columns(to_west, to_east)
    for pairs in (lat_pairs(1, 0), lat_pairs(3, 0), lat_pairs(0, 1)):
        part = part + lax.ppermute(part, "lat", pairs)
    part, west, east = lax.optimization_barrier((part, west, east))
    mine = swap(jnp.broadcast_to(part[None], (16, piece, COLS))).reshape(half, COLS)
    done = finish(south, north, west, east)
    mine, done = lax.optimization_barrier((mine, done))
    other = lax.ppermute(mine, "lon", core_pairs())
    total = jnp.concatenate([jnp.where(odd, other, mine), jnp.where(odd, mine, other)], axis=0)
    return total, done


def per_device(
    sea_state,
    conv_kernel,
    conv_bias,
    norm_gain,
    norm_shift,
    w_in,
    b_in,
    w_out,
    b_out,
    layer_scale,
    sea_mask,
    cotangent,
):
    lat_size, lon_size = lax.axis_size("lat"), lax.axis_size("lon")
    lat = lax.axis_index("lat")
    flags = jnp.stack([(lat % 2 == 0).astype(jnp.int32), (lat == lat_size - 1).astype(jnp.int32)])
    rows_shape = jax.ShapeDtypeStruct((ROWS, CH, COLS), f32)
    block = jax.ShapeDtypeStruct((CH, ROWS, COLS), bf16)

    top = jnp.transpose(sea_state[:, ROWS - 3 :, :].astype(f32), (1, 0, 2))
    bottom = jnp.transpose(sea_state[:, :3, :].astype(f32), (1, 0, 2))
    mask = sea_mask.astype(f32)
    tall = pltpu.VMEM((CH * ROWS, COLS), f32)
    state_rows, cot_rows = call(
        prepare_body,
        (rows_shape, rows_shape),
        (sea_state, cotangent, mask),
        [tall, tall],
        flops=1 << 20,
        nbytes=3 << 20,
        name="prepare",
    )
    weights = jnp.broadcast_to(conv_kernel.astype(f32).T[:, :, None], (49, CH, COLS))
    chan = jnp.stack([conv_bias, norm_gain, norm_shift, b_out, layer_scale]).astype(f32)
    chan = jnp.broadcast_to(chan[:, :, None], (5, CH, COLS))
    bias_in = jnp.broadcast_to(b_in.astype(f32)[:, None], (HID, COLS))

    from_a, from_b = exchange_rows(flags, top, bottom)
    north, south, to_west, to_east = settle_edges(flags, from_a, from_b, state_rows)
    halo = (south, north) + exchange_columns(to_west, to_east)
    shifted = pltpu.VMEM((7, PAD, CH, COLS), f32)
    flat = pltpu.VMEM((CH, COLS), f32)
    new_rows, conv_grad, sums = call(
        main_body,
        (rows_shape, rows_shape, jax.ShapeDtypeStruct((320, COLS), f32)),
        (state_rows,)
        + halo
        + (cot_rows, mask, weights, chan, bias_in, w_in, w_in.T, w_out, w_out.T),
        [
            shifted,
            pltpu.VMEM((ROWS, CH, COLS), f32),
            pltpu.VMEM((CH, HID), f32),
            pltpu.VMEM((HID, CH), f32),
            pltpu.VMEM((HID, COLS), f32),
            flat,
            flat,
            flat,
            flat,
        ],
        flops=1 << 30,
        nbytes=8 << 20,
        name="main",
    )

    def finish(*halo):
        return call(
            spread_body,
            (block, block),
            (flags, conv_grad) + halo + (weights, cot_rows, new_rows),
            [shifted, tall],
            smem_first=True,
            flops=1 << 26,
            nbytes=6 << 20,
            name="spread",
        )

    total, (state_grad, new_state) = reduce_and_spread(sums, flags, conv_grad, finish)
    grad_scale = 1.0 / math.sqrt(ROWS * lat_size * COLS * lon_size)
    kernel_grad, w_in_grad, w_out_grad, b_in_grad, channel_grads = call(
        functools.partial(unpack_body, scale=grad_scale),
        (
            jax.ShapeDtypeStruct((CH, 49), f32),
            jax.ShapeDtypeStruct((CH, HID), f32),
            jax.ShapeDtypeStruct((HID, CH), f32),
            jax.ShapeDtypeStruct((1, HID), f32),
            jax.ShapeDtypeStruct((5, CH), f32),
        ),
        (total,),
        flops=1 << 17,
        nbytes=1 << 18,
        name="unpack",
    )
    return (
        new_state,
        state_grad,
        kernel_grad,
        w_in_grad,
        w_out_grad,
        b_in_grad.reshape(HID),
        channel_grads,
    )


def solution(mesh):
    grid = P(None, "lat", "lon")
    placed = (grid,) + (P(),) * 9 + (P("lat", "lon"), grid)
    return jax.shard_map(
        per_device,
        mesh=mesh,
        in_specs=placed,
        out_specs=(grid, grid, P(), P(), P(), P(), P()),
        check_vma=False,
    )
```

```python
import functools
import math

import jax
import jax.numpy as jnp
import numpy as np
from jax import lax
from jax.experimental import pallas as pl
from jax.experimental.pallas import tpu as pltpu
from jax.sharding import PartitionSpec as P

slope_coef = 0.044715
tanh_scale = math.sqrt(2.0 / math.pi)
ln_epsilon = 1e-06
f32, bf16 = jnp.float32, jnp.bfloat16

CH, ROWS, COLS, HID = 64, 32, 128, 256
AXES = ("lat", "lon")
VM = pl.BlockSpec(memory_space=pltpu.VMEM)
SM = pl.BlockSpec(memory_space=pltpu.SMEM)
PITCH = ROWS + 1
SPAN = 40
NEAR = 9
PART = 16


def call(body, out_shape, args, scratch=(), smem_first=False, flops=0, nbytes=0, name=None, mib=8):
    specs = [VM] * len(args)
    if smem_first:
        specs[0] = SM
    return pl.pallas_call(
        body,
        out_shape=out_shape,
        in_specs=specs,
        out_specs=jax.tree.map(lambda _: VM, out_shape),
        scratch_shapes=list(scratch),
        compiler_params=pltpu.CompilerParams(vmem_limit_bytes=mib * 1024 * 1024),
        cost_estimate=pl.CostEstimate(flops=flops, bytes_accessed=nbytes, transcendentals=0),
        name=name,
    )(*args)


def iota(shape, dim):
    return lax.broadcasted_iota(jnp.int32, shape, dim)


def by_channel(step, group=8, count=CH):
    def run(i, carry):
        for j in range(group):
            step(i * group, j)
        return carry

    lax.fori_loop(0, count // group, run, 0)


def pitched(ref, base, j):
    return ref.at[pl.ds(pl.multiple_of(base * PITCH, 8) + j * PITCH, ROWS), :]


def row_of(ref, r):
    return ref.at[pl.ds(r, CH, stride=PITCH), :]


def near_fill(near, north, south):
    near[...] = jnp.zeros_like(near)
    count = north.shape[1]
    for g in range(3):
        near[pl.ds(g, count, stride=NEAR), :] = north[g]
        near[pl.ds(5 + g, count, stride=NEAR), :] = south[g]


def edges_body(flags, from_a, from_b, own, north, south, to_west, to_east, near):
    even = flags[0] == 1
    on_top = flags[1] == 1
    for g in range(3):
        south[g] = jnp.where(even, from_b[g], from_a[g])

    @pl.when(jnp.logical_not(on_top))
    def _():
        for g in range(3):
            north[g] = jnp.where(even, from_a[g], from_b[g])

    @pl.when(on_top)
    def _():
        back = COLS - 1 - iota((CH, COLS), 1)
        for g in range(3):
            got = jnp.where(even, from_a[2 - g], from_b[2 - g])
            north[g] = jnp.take_along_axis(got, back, axis=1)

    near_fill(near, north, south)
    lane = iota((SPAN, COLS), 1)
    for t in range(2):
        west = jnp.zeros((SPAN, COLS), f32)
        east = jnp.zeros((SPAN, COLS), f32)
        for m in range(32):
            k = 32 * t + m
            mine = own[k * PITCH : k * PITCH + ROWS, :] if len(own.shape) == 2 else own[k].astype(f32)
            value = jnp.concatenate([mine, near[k * NEAR : k * NEAR + 8, :]], axis=0)
            here = jnp.logical_and(lane >= 3 * m, lane < 3 * m + 3)
            west = jnp.where(here, pltpu.roll(value, 3 * m, 1) if m else value, west)
            east = jnp.where(here, pltpu.roll(value, 3 * m + 3, 1), east)
        to_west[t] = west
        to_east[t] = east


def build_shifted(shifted, own, near, west, east, count, find):
    lane = iota((SPAN, COLS), 1)
    blank = jnp.zeros((8, COLS), f32)

    def step(base, j):
        k = base + j
        value = jnp.concatenate([own(base, j), near[pl.ds(base * NEAR + j * NEAR, 8), :]], axis=0)
        t, m = find(base, j)
        from_west = pltpu.roll(west[t], 125 - 3 * m, 1)
        from_east = pltpu.roll(east[t], lax.rem(COLS - 3 * m, COLS), 1)
        for b in range(7):
            off = b - 3
            if off == 0:
                v = value
            elif off < 0:
                v = pltpu.roll(jnp.where(lane >= COLS + off, from_west, value), -off, 1)
            else:
                v = pltpu.roll(jnp.where(lane < off, from_east, value), COLS - off, 1)
            p, g = divmod(b, 2)
            mine, other = 128 * p + 64 * g, 128 * p + 64 * (1 - g)
            edge = v[ROWS:]
            shifted[k, mine : mine + 32, :] = v[:ROWS].astype(bf16)
            shifted[k, mine + 32 : mine + 48, :] = jnp.concatenate([edge, blank], 0).astype(bf16)
            shifted[k, other + 48 : other + 64, :] = jnp.concatenate([blank, edge], 0).astype(bf16)
        zero = jnp.zeros((16, COLS), bf16)
        for spot in (384 + 48, 384 + 64, 384 + 80, 384 + 96):
            shifted[k, spot : spot + 16, :] = zero

    by_channel(step, 4, count)


def banded(taps, base, j):
    rows = taps[pl.ds(pl.multiple_of(base, 8), 8), :]
    tiles = []
    for p in range(4):
        row = jnp.broadcast_to(rows[j : j + 1, 128 * p : 128 * p + 128], (8, COLS))
        parts = [pltpu.roll(row, 8 * i, 1, stride=1, stride_axis=0) for i in range(4)]
        tiles.append(jnp.concatenate(parts, axis=0))
    return jnp.concatenate(tiles, axis=1)


def main_body(
    state,
    south,
    north,
    west,
    east,
    cot,
    mask,
    taps,
    chan,
    w_in,
    w_in_t,
    w_out,
    w_out_t,
    delta,
    conv_grad,
    top,
    bottom,
    sums,
    shifted,
    near,
    conv_out,
    cot_rows,
    grad_back,
    win_acc,
    wout_acc,
    gain_acc,
    shift_acc,
    obias_acc,
    scale_acc,
    taps_acc,
):
    near_fill(near, north, south)
    build_shifted(
        shifted,
        lambda base, j: state[base + j].astype(f32),
        near,
        west,
        east,
        CH,
        lambda base, j: (base // 32, lax.rem(base, 32) + j),
    )

    def conv_step(base, j):
        k = base + j
        out = jnp.dot(banded(taps, base, j).astype(bf16), shifted[k], preferred_element_type=f32)
        pitched(conv_out, base, j)[...] = out
        pitched(cot_rows, base, j)[...] = cot[k].astype(f32) * mask[...]

    by_channel(conv_step)

    for acc in (win_acc, wout_acc, gain_acc, shift_acc, obias_acc, scale_acc):
        acc[...] = jnp.zeros_like(acc)

    def wide(x):
        return jnp.concatenate([x, x], axis=1)

    def fold(x):
        return x[:, :COLS] + x[:, COLS:]

    def pair(ref, r):
        return jnp.concatenate([row_of(ref, r)[...], row_of(ref, r + 1)[...]], axis=1)

    def mean(x):
        return jnp.sum(x, axis=0, keepdims=True) * (1.0 / CH)

    cells = (((1,), (1,)), ((), ()))
    ones = jnp.where(iota((16, 2 * COLS), 0) == 0, 1.0, 0.0).astype(bf16)

    def point_step(i, carry):
        r = 2 * i
        conv_bias, gain, shift, out_bias, scale = (wide(chan[n]) for n in range(5))
        x = pair(conv_out, r) + conv_bias
        centre = x - mean(x)
        inv_std = lax.rsqrt(mean(centre * centre) + ln_epsilon)
        unit = centre * inv_std
        normed = jnp.concatenate([(unit * gain + shift).astype(bf16), ones], axis=0)
        masked_cot = pair(cot_rows, r)
        mixed_grad = (scale * masked_cot).astype(bf16)
        u = jnp.dot(w_in_t[...], normed, preferred_element_type=f32)
        half_grad = jnp.dot(w_out[...], mixed_grad, preferred_element_type=f32)
        bent = (tanh_scale * slope_coef) * (u * u)
        t = jnp.tanh(u * (tanh_scale + bent))
        s = 1.0 + t
        hidden = (u * s).astype(bf16)
        slope = s + s * (1.0 - t) * (u * (tanh_scale + 3.0 * bent))
        pre_grad = (half_grad * slope).astype(bf16)
        mixed = jnp.dot(w_out_t[...], hidden, preferred_element_type=f32) + out_bias
        normed_grad = jnp.dot(w_in[...], pre_grad, preferred_element_type=f32)
        win_acc[...] += lax.dot_general(normed, pre_grad, cells, preferred_element_type=f32)
        wout_acc[...] += lax.dot_general(hidden, mixed_grad, cells, preferred_element_type=f32)
        change = scale * mixed
        row_of(delta, r)[...] = change[:, :COLS]
        row_of(delta, r + 1)[...] = change[:, COLS:]
        scale_acc[...] += fold(masked_cot * mixed)
        obias_acc[...] += fold(mixed_grad.astype(f32))
        slant = normed_grad * unit
        gain_acc[...] += fold(slant)
        shift_acc[...] += fold(normed_grad)
        q = normed_grad * gain
        grad = inv_std * (q - mean(q) - unit * mean(slant * gain))
        for n in range(2):
            part = grad[:, n * COLS : (n + 1) * COLS]
            row_of(conv_grad, r + n)[...] = part
            row_of(grad_back, ROWS - 1 - r - n)[...] = part
        return carry

    lax.fori_loop(0, ROWS // 2, point_step, 0, unroll=2)

    for g in range(3):
        bottom[g] = row_of(conv_grad, g)[...]
        top[g] = row_of(conv_grad, ROWS - 3 + g)[...]

    def grad_step(base, j):
        k = base + j
        back = pitched(grad_back, base, j)[...]
        prod = lax.dot_general(back.astype(bf16), shifted[k], cells, preferred_element_type=f32)
        for p in range(4):
            acc = None
            for i in range(4):
                tile = prod[8 * i : 8 * i + 8, 128 * p : 128 * p + 128]
                tile = pltpu.roll(tile, 8 * i, 1, stride=1, stride_axis=0)
                acc = tile if acc is None else acc + tile
            taps_acc[p, pl.ds(k, 1), :] = jnp.sum(acc, axis=0, keepdims=True)

    by_channel(grad_step)

    lane = iota((CH, COLS), 1)

    def total(x):
        return jnp.broadcast_to(jnp.sum(x, axis=1, keepdims=True), (CH, COLS))

    bias = row_of(conv_grad, 0)[...]
    for r in range(1, ROWS):
        bias = bias + row_of(conv_grad, r)[...]
    small = (bias, gain_acc[...], shift_acc[...], obias_acc[...], scale_acc[...])
    tail = jnp.zeros((CH, COLS), f32)
    for n, x in enumerate(small):
        tail = jnp.where(lane == n, total(x), tail)
    used = jnp.logical_and(lax.rem(lane, 64) >= 28, lax.rem(lane, 64) < 35)
    for p in range(4):
        moved = jnp.where(used, taps_acc[p], 0.0)
        tail = tail + (pltpu.roll(moved, 7 * p, 1) if p else moved)
    extra = win_acc[CH : CH + 8, :]
    turned = jnp.transpose(
        jnp.concatenate([extra[:, :COLS], extra[:, COLS:], jnp.zeros((112, COLS), f32)], axis=0)
    )
    for n in range(4):
        part = turned[CH * (n % 2) : CH * (n % 2) + CH, :]
        tail = jnp.where(lane == 5 + n, pltpu.roll(part, (5 + n - 8 * (n // 2)) % COLS, 1), tail)
    sums[0:64, :] = win_acc[0:CH, :COLS]
    sums[64:128, :] = win_acc[0:CH, COLS:]
    sums[128:256, :] = 0.5 * jnp.concatenate([wout_acc[0:128, :], wout_acc[128:256, :]], axis=1)
    sums[256:320, :] = tail


def spread_body(
    flags,
    conv_grad,
    south,
    north,
    west,
    east,
    taps,
    turned_taps,
    cot,
    mask,
    state,
    delta,
    *rest,
    first,
):
    state_grad, new_state, shifted, near = rest[-4:]
    near_fill(near, north, south)
    build_shifted(
        shifted,
        lambda base, j: pitched(conv_grad, base, j)[...],
        near,
        west,
        east,
        PART,
        lambda base, j: (0, first + base + j),
    )
    on_top = flags[1] == 1
    spot = lax.rem(iota((ROWS, 512), 1), 64)
    beyond = jnp.logical_and(on_top, jnp.logical_and(spot >= 32, spot < 35))

    def step(base, j):
        k = base + j
        band = jnp.where(beyond, banded(taps, base, j), banded(turned_taps, base, j))
        out = jnp.dot(band.astype(bf16), shifted[k], preferred_element_type=f32)
        ocean = mask[...]
        state_grad[k] = (cot[k].astype(f32) * ocean + out).astype(bf16)
        new = ocean * (state[k].astype(f32) + pitched(delta, base, j)[...])
        new_state[k] = new.astype(bf16)

    by_channel(step, 8, PART)


def spread_part(c, held, flags, conv_grad, south, north, west, east, taps, turned, cot, mask, state, delta):
    tall = pl.BlockSpec((PART * PITCH, COLS), lambda _: (c, 0))
    slab = pl.BlockSpec((3, PART, COLS), lambda _: (0, c, 0))
    side = pl.BlockSpec((1, SPAN, COLS), lambda _: (c * PART // 32, 0, 0))
    band = pl.BlockSpec((PART, 512), lambda _: (c, 0))
    block = pl.BlockSpec((PART, ROWS, COLS), lambda _: (c, 0, 0))
    shape = jax.ShapeDtypeStruct((CH, ROWS, COLS), bf16)
    args = (flags, conv_grad, south, north, west, east, taps, turned, cot, mask, state, delta)
    whole = pl.BlockSpec((ROWS, COLS), lambda _: (0, 0))
    specs = [SM, tall, slab, slab, side, side, band, band, block, whole, block, tall]
    kept = [pl.BlockSpec(memory_space=pl.ANY)] * len(held)
    return pl.pallas_call(
        functools.partial(spread_body, first=c * PART % 32),
        grid=(1,),
        out_shape=(shape, shape),
        in_specs=specs + kept,
        out_specs=(block, block),
        scratch_shapes=[
            pltpu.VMEM((PART, 512, COLS), bf16),
            pltpu.VMEM((PART * NEAR, COLS), f32),
        ],
        input_output_aliases={len(args) + n: n for n in range(len(held))},
        compiler_params=pltpu.CompilerParams(vmem_limit_bytes=16 * 1024 * 1024),
        cost_estimate=pl.CostEstimate(flops=1 << 24, bytes_accessed=3 << 20, transcendentals=0),
        name="spread",
    )(*args, *held)


def unpack_body(
    sums, pick, kernel_grad, w_in_grad, w_out_grad, b_in_grad, channel_grads, *, scale
):
    w_in_grad[:, :COLS] = sums[0:64, :] * scale
    w_in_grad[:, COLS:] = sums[64:128, :] * scale
    packed = jnp.transpose(sums[128:256, :] * scale)
    w_out_grad[:, :COLS] = packed[:CH]
    w_out_grad[:, COLS:] = packed[CH:]
    tail = sums[256:320, :] * scale
    turned = jnp.transpose(jnp.concatenate([tail, tail], axis=0))
    kernel_grad[...] = jnp.dot(
        pick[...], turned, preferred_element_type=f32, precision=lax.Precision.HIGHEST
    )[:, :CH]
    channel_grads[...] = turned[0:5, :CH]
    for n in range(4):
        b_in_grad[:, CH * n : CH * n + CH] = turned[5 + n : 6 + n, :CH]


def tap_tables():
    place = np.zeros((49, 512), np.float32)
    turned = np.zeros((49, 512), np.float32)
    pick = np.zeros((49, COLS), np.float32)
    for a in range(7):
        for b in range(7):
            p, g = divmod(b, 2)
            spot = 128 * p + (64 * g + a - 3) % 128
            place[7 * a + b, spot] = 1.0
            turned[48 - (7 * a + b), spot] = 1.0
            pick[7 * a + b, 28 + 7 * p + a + 64 * g] = 1.0
    return place, turned, pick


def row_pairs(lat_size, lon_size):
    first, second = [], []
    for i in range(lat_size):
        for j in range(lon_size):
            me = i * lon_size + j
            first.append((me, (i ^ 1) * lon_size + j))
            if i == lat_size - 1:
                second.append((me, i * lon_size + lon_size - 1 - j))
            elif i > 0:
                other = i + 1 if i % 2 else i - 1
                second.append((me, other * lon_size + j))
    return first, second


def exchange_rows(flags, top, bottom):
    first, second = row_pairs(lax.axis_size("lat"), lax.axis_size("lon"))
    even = flags[0] == 1
    from_a = lax.ppermute(jnp.where(even, top, bottom), AXES, first)
    from_b = lax.ppermute(jnp.where(even, bottom, top), AXES, second)
    return from_a, from_b


def settle_edges(flags, from_a, from_b, rows):
    slab = jax.ShapeDtypeStruct((3, CH, COLS), f32)
    flat = jax.ShapeDtypeStruct((2, SPAN, COLS), f32)
    return call(
        edges_body,
        (slab, slab, flat, flat),
        (flags, from_a, from_b, rows),
        [pltpu.VMEM((CH * NEAR, COLS), f32)],
        smem_first=True,
        flops=1 << 20,
        nbytes=1 << 21,
        name="edges",
    )


def exchange_columns(to_west, to_east):
    lon_size = lax.axis_size("lon")
    up = [(j, (j + 1) % lon_size) for j in range(lon_size)]
    down = [(k, j) for j, k in up]
    west = lax.ppermute(to_east, "lon", up)
    east = lax.ppermute(to_west, "lon", down)
    return west, east


def core_pairs():
    return [(i, i ^ 1) for i in range(32)]


def chip_pairs(flip_x, flip_y, flip_z):
    pairs = []
    for i in range(256):
        lat, lon = divmod(i, 32)
        x = ((lat >> 2) * 2 + (lon >> 4)) ^ flip_x
        y = (lat & 3) ^ flip_y
        z = ((lon >> 1) & 7) ^ flip_z
        pairs.append((i, ((x >> 1) * 4 + y) * 32 + (x & 1) * 16 + z * 2 + (lon & 1)))
    return pairs


def tie(*values):
    return lax.optimization_barrier(values)


def reduce_and_spread(sums, flags, conv_grad, top, bottom, finish):
    odd = lax.rem(lax.axis_index("lon"), 2) == 1
    half = sums.shape[0] // 2
    low, high = sums[:half], sums[half:]
    mine = jnp.where(odd, high, low) + lax.ppermute(jnp.where(odd, low, high), "lon", core_pairs())
    from_a, from_b = exchange_rows(flags, top, bottom)

    def hop(x, *flips):
        return x + lax.ppermute(x, AXES, chip_pairs(*flips))

    mine, from_a, from_b = tie(hop(mine, 1, 0, 0), from_a, from_b)
    north, south, to_west, to_east = settle_edges(flags, from_a, from_b, conv_grad)
    mine, to_west, to_east = tie(hop(mine, 3, 0, 0), to_west, to_east)
    west, east = exchange_columns(to_west, to_east)
    mine, west, east = tie(hop(mine, 0, 1, 0), west, east)
    done = ()
    for c, flips in enumerate(((0, 3, 0), (0, 0, 1), (0, 0, 2), (0, 0, 4))):
        done = finish(c, done, south, north, west, east)
        mine, *done = tie(hop(mine, *flips), *done)
    other = lax.ppermute(mine, "lon", core_pairs())
    total = jnp.concatenate([jnp.where(odd, other, mine), jnp.where(odd, mine, other)], axis=0)
    return total, done


def per_device(
    sea_state,
    conv_kernel,
    conv_bias,
    norm_gain,
    norm_shift,
    w_in,
    b_in,
    w_out,
    b_out,
    layer_scale,
    sea_mask,
    cotangent,
):
    lat_size, lon_size = lax.axis_size("lat"), lax.axis_size("lon")
    lat = lax.axis_index("lat")
    flags = jnp.stack([(lat % 2 == 0).astype(jnp.int32), (lat == lat_size - 1).astype(jnp.int32)])
    top = jnp.transpose(sea_state[:, ROWS - 3 :, :].astype(f32), (1, 0, 2))
    bottom = jnp.transpose(sea_state[:, :3, :].astype(f32), (1, 0, 2))
    from_a, from_b = exchange_rows(flags, top, bottom)
    mask = sea_mask.astype(f32)
    place, turned, pick = (jnp.asarray(x) for x in tap_tables())
    taps = jnp.dot(conv_kernel, place.astype(bf16), preferred_element_type=f32)
    turned_taps = jnp.dot(conv_kernel, turned.astype(bf16), preferred_element_type=f32)
    chan = jnp.stack([conv_bias, norm_gain, norm_shift, b_out, layer_scale]).astype(f32)
    chan = jnp.broadcast_to(chan[:, :, None], (5, CH, COLS))
    w_in_t = jnp.concatenate([w_in.T, b_in[:, None], jnp.zeros((HID, 15), bf16)], axis=1)
    half_out = (w_out.astype(f32) * 0.5).astype(bf16)
    north, south, to_west, to_east = settle_edges(flags, from_a, from_b, sea_state)
    halo = (south, north) + exchange_columns(to_west, to_east)
    shifted = pltpu.VMEM((CH, 512, COLS), bf16)
    near = pltpu.VMEM((CH * NEAR, COLS), f32)
    flat = pltpu.VMEM((CH, COLS), f32)
    tall_shape = (CH * PITCH, COLS)
    tall = pltpu.VMEM(tall_shape, f32)
    slab = jax.ShapeDtypeStruct((3, CH, COLS), f32)
    delta, conv_grad, top, bottom, sums = call(
        main_body,
        (
            jax.ShapeDtypeStruct(tall_shape, f32),
            jax.ShapeDtypeStruct(tall_shape, f32),
            slab,
            slab,
            jax.ShapeDtypeStruct((320, COLS), f32),
        ),
        (sea_state,)
        + halo
        + (cotangent, mask, taps, chan, w_in, w_in_t, half_out, half_out.T),
        [
            shifted,
            near,
            tall,
            tall,
            tall,
            pltpu.VMEM((CH + 16, HID), f32),
            pltpu.VMEM((HID, CH), f32),
            flat,
            flat,
            flat,
            flat,
            pltpu.VMEM((4, CH, COLS), f32),
        ],
        flops=1 << 30,
        nbytes=8 << 20,
        name="main",
        mib=28,
    )

    def finish(c, held, *halo):
        rest = (taps, turned_taps, cotangent, mask, sea_state, delta)
        return spread_part(c, held, flags, conv_grad, *halo, *rest)

    total, (state_grad, new_state) = reduce_and_spread(
        sums, flags, conv_grad, top, bottom, finish
    )
    grad_scale = 1.0 / math.sqrt(ROWS * lat_size * COLS * lon_size)
    kernel_grad, w_in_grad, w_out_grad, b_in_grad, channel_grads = call(
        functools.partial(unpack_body, scale=grad_scale),
        (
            jax.ShapeDtypeStruct((49, CH), f32),
            jax.ShapeDtypeStruct((CH, HID), f32),
            jax.ShapeDtypeStruct((CH, HID), f32),
            jax.ShapeDtypeStruct((1, HID), f32),
            jax.ShapeDtypeStruct((5, CH), f32),
        ),
        (total, pick),
        flops=1 << 17,
        nbytes=1 << 18,
        name="unpack",
    )
    return (
        new_state,
        state_grad,
        kernel_grad.T,
        w_in_grad,
        w_out_grad.T,
        b_in_grad.reshape(HID),
        channel_grads,
    )


def solution(mesh):
    grid = P(None, "lat", "lon")
    placed = (grid,) + (P(),) * 9 + (P("lat", "lon"), grid)
    return jax.shard_map(
        per_device,
        mesh=mesh,
        in_specs=placed,
        out_specs=(grid, grid, P(), P(), P(), P(), P()),
        check_vma=False,
    )
```

```python
import functools
import math

import jax
import jax.numpy as jnp
import numpy as np
from jax import lax
from jax.experimental import pallas as pl
from jax.experimental.pallas import tpu as pltpu
from jax.sharding import PartitionSpec as P

slope_coef = 0.044715
tanh_scale = math.sqrt(2.0 / math.pi)
ln_epsilon = 1e-06
f32, bf16 = jnp.float32, jnp.bfloat16

CH, ROWS, COLS, HID = 64, 32, 128, 256
AXES = ("lat", "lon")
VM = pl.BlockSpec(memory_space=pltpu.VMEM)
SM = pl.BlockSpec(memory_space=pltpu.SMEM)
PITCH = ROWS + 1
SPAN = 40
NEAR = 9
PART = 16
TOGETHER = 8


def call(body, out_shape, args, scratch=(), smem_first=False, flops=0, nbytes=0, name=None, mib=8):
    specs = [VM] * len(args)
    if smem_first:
        specs[0] = SM
    return pl.pallas_call(
        body,
        out_shape=out_shape,
        in_specs=specs,
        out_specs=jax.tree.map(lambda _: VM, out_shape),
        scratch_shapes=list(scratch),
        compiler_params=pltpu.CompilerParams(vmem_limit_bytes=mib * 1024 * 1024),
        cost_estimate=pl.CostEstimate(flops=flops, bytes_accessed=nbytes, transcendentals=0),
        name=name,
    )(*args)


def iota(shape, dim):
    return lax.broadcasted_iota(jnp.int32, shape, dim)


def by_channel(step, group=8, count=CH):
    def run(i, carry):
        for j in range(group):
            step(i * group, j)
        return carry

    lax.fori_loop(0, count // group, run, 0)


def pitched(ref, base, j):
    return ref.at[pl.ds(pl.multiple_of(base * PITCH, 8) + j * PITCH, ROWS), :]


def row_of(ref, r):
    return ref.at[pl.ds(r, CH, stride=PITCH), :]


def near_fill(near, north, south):
    near[...] = jnp.zeros_like(near)
    count = north.shape[1]
    for g in range(3):
        near[pl.ds(g, count, stride=NEAR), :] = north[g]
        near[pl.ds(5 + g, count, stride=NEAR), :] = south[g]


def edges_body(flags, from_a, from_b, own, north, south, to_west, to_east, near):
    even = flags[0] == 1
    on_top = flags[1] == 1
    for g in range(3):
        south[g] = jnp.where(even, from_b[g], from_a[g])

    @pl.when(jnp.logical_not(on_top))
    def _():
        for g in range(3):
            north[g] = jnp.where(even, from_a[g], from_b[g])

    @pl.when(on_top)
    def _():
        back = COLS - 1 - iota((CH, COLS), 1)
        for g in range(3):
            got = jnp.where(even, from_a[2 - g], from_b[2 - g])
            north[g] = jnp.take_along_axis(got, back, axis=1)

    near_fill(near, north, south)
    lane = iota((SPAN, COLS), 1)
    for t in range(2):
        west = jnp.zeros((SPAN, COLS), f32)
        east = jnp.zeros((SPAN, COLS), f32)
        for m in range(32):
            k = 32 * t + m
            mine = own[k * PITCH : k * PITCH + ROWS, :] if len(own.shape) == 2 else own[k].astype(f32)
            value = jnp.concatenate([mine, near[k * NEAR : k * NEAR + 8, :]], axis=0)
            here = jnp.logical_and(lane >= 3 * m, lane < 3 * m + 3)
            west = jnp.where(here, pltpu.roll(value, 3 * m, 1) if m else value, west)
            east = jnp.where(here, pltpu.roll(value, 3 * m + 3, 1), east)
        to_west[t] = west
        to_east[t] = east


def build_shifted(shifted, own, near, west, east, count, find):
    lane = iota((SPAN, COLS), 1)
    blank = jnp.zeros((8, COLS), f32)

    def step(base, j):
        k = base + j
        value = jnp.concatenate([own(base, j), near[pl.ds(base * NEAR + j * NEAR, 8), :]], axis=0)
        t, m = find(base, j)
        from_west = pltpu.roll(west[t], 125 - 3 * m, 1)
        from_east = pltpu.roll(east[t], lax.rem(COLS - 3 * m, COLS), 1)
        for b in range(7):
            off = b - 3
            if off == 0:
                v = value
            elif off < 0:
                v = pltpu.roll(jnp.where(lane >= COLS + off, from_west, value), -off, 1)
            else:
                v = pltpu.roll(jnp.where(lane < off, from_east, value), COLS - off, 1)
            p, g = divmod(b, 2)
            mine, other = 128 * p + 64 * g, 128 * p + 64 * (1 - g)
            edge = v[ROWS:]
            shifted[k, mine : mine + 32, :] = v[:ROWS].astype(bf16)
            shifted[k, mine + 32 : mine + 48, :] = jnp.concatenate([edge, blank], 0).astype(bf16)
            shifted[k, other + 48 : other + 64, :] = jnp.concatenate([blank, edge], 0).astype(bf16)
        zero = jnp.zeros((16, COLS), bf16)
        for spot in (384 + 48, 384 + 64, 384 + 80, 384 + 96):
            shifted[k, spot : spot + 16, :] = zero

    by_channel(step, 4, count)


def banded(taps, base, j):
    rows = taps[pl.ds(pl.multiple_of(base, 8), 8), :]
    tiles = []
    for p in range(4):
        row = jnp.broadcast_to(rows[j : j + 1, 128 * p : 128 * p + 128], (8, COLS))
        parts = [pltpu.roll(row, 8 * i, 1, stride=1, stride_axis=0) for i in range(4)]
        tiles.append(jnp.concatenate(parts, axis=0))
    return jnp.concatenate(tiles, axis=1)


def main_body(
    state,
    south,
    north,
    west,
    east,
    cot,
    mask,
    taps,
    chan,
    w_in,
    w_in_t,
    w_out,
    w_out_t,
    delta,
    conv_grad,
    top,
    bottom,
    sums,
    shifted,
    near,
    conv_out,
    cot_rows,
    grad_back,
    win_acc,
    wout_acc,
    gain_acc,
    shift_acc,
    obias_acc,
    scale_acc,
    taps_acc,
):
    near_fill(near, north, south)
    build_shifted(
        shifted,
        lambda base, j: state[base + j].astype(f32),
        near,
        west,
        east,
        CH,
        lambda base, j: (base // 32, lax.rem(base, 32) + j),
    )

    def conv_step(base, j):
        k = base + j
        out = jnp.dot(banded(taps, base, j).astype(bf16), shifted[k], preferred_element_type=f32)
        pitched(conv_out, base, j)[...] = out
        pitched(cot_rows, base, j)[...] = cot[k].astype(f32) * mask[...]

    by_channel(conv_step)

    for acc in (win_acc, wout_acc, gain_acc, shift_acc, obias_acc, scale_acc):
        acc[...] = jnp.zeros_like(acc)

    def wide(x):
        return jnp.concatenate([x] * TOGETHER, axis=1)

    def fold(x):
        return sum(x[:, n * COLS : (n + 1) * COLS] for n in range(TOGETHER))

    def pair(ref, r):
        return jnp.concatenate([row_of(ref, r + n)[...] for n in range(TOGETHER)], axis=1)

    def mean(x):
        return jnp.sum(x, axis=0, keepdims=True) * (1.0 / CH)

    cells = (((1,), (1,)), ((), ()))
    ones = jnp.where(iota((16, TOGETHER * COLS), 0) == 0, 1.0, 0.0).astype(bf16)

    def point_step(i, carry):
        r = TOGETHER * i
        conv_bias, gain, shift, out_bias, scale = (wide(chan[n]) for n in range(5))
        x = pair(conv_out, r) + conv_bias
        centre = x - mean(x)
        inv_std = lax.rsqrt(mean(centre * centre) + ln_epsilon)
        unit = centre * inv_std
        normed = jnp.concatenate([(unit * gain + shift).astype(bf16), ones], axis=0)
        masked_cot = pair(cot_rows, r)
        mixed_grad = (scale * masked_cot).astype(bf16)
        u = jnp.dot(w_in_t[...], normed, preferred_element_type=f32)
        half_grad = jnp.dot(w_out[...], mixed_grad, preferred_element_type=f32)
        bent = (tanh_scale * slope_coef) * (u * u)
        t = jnp.tanh(u * (tanh_scale + bent))
        s = 1.0 + t
        hidden = (u * s).astype(bf16)
        slope = s * (1.0 + (1.0 - t) * (u * (tanh_scale + 3.0 * bent)))
        pre_grad = (half_grad * slope).astype(bf16)
        mixed = jnp.dot(w_out_t[...], hidden, preferred_element_type=f32) + out_bias
        normed_grad = jnp.dot(w_in[...], pre_grad, preferred_element_type=f32)
        win_acc[...] += lax.dot_general(normed, pre_grad, cells, preferred_element_type=f32)
        wout_acc[...] += lax.dot_general(hidden, mixed_grad, cells, preferred_element_type=f32)
        change = scale * mixed
        for n in range(TOGETHER):
            row_of(delta, r + n)[...] = change[:, n * COLS : (n + 1) * COLS]
        scale_acc[...] += fold(masked_cot * mixed)
        obias_acc[...] += fold(mixed_grad.astype(f32))
        slant = normed_grad * unit
        gain_acc[...] += fold(slant)
        shift_acc[...] += fold(normed_grad)
        q = normed_grad * gain
        grad = inv_std * (q - mean(q) - unit * mean(slant * gain))
        for n in range(TOGETHER):
            part = grad[:, n * COLS : (n + 1) * COLS]
            row_of(conv_grad, r + n)[...] = part
            row_of(grad_back, ROWS - 1 - r - n)[...] = part
        return carry

    lax.fori_loop(0, ROWS // TOGETHER, point_step, 0)

    for g in range(3):
        bottom[g] = row_of(conv_grad, g)[...]
        top[g] = row_of(conv_grad, ROWS - 3 + g)[...]

    def grad_step(base, j):
        k = base + j
        back = pitched(grad_back, base, j)[...]
        prod = lax.dot_general(back.astype(bf16), shifted[k], cells, preferred_element_type=f32)
        for p in range(4):
            acc = None
            for i in range(4):
                tile = prod[8 * i : 8 * i + 8, 128 * p : 128 * p + 128]
                tile = pltpu.roll(tile, 8 * i, 1, stride=1, stride_axis=0)
                acc = tile if acc is None else acc + tile
            taps_acc[p, pl.ds(k, 1), :] = jnp.sum(acc, axis=0, keepdims=True)

    by_channel(grad_step, 16)

    lane = iota((CH, COLS), 1)

    def total(x):
        return jnp.broadcast_to(jnp.sum(x, axis=1, keepdims=True), (CH, COLS))

    bias = row_of(conv_grad, 0)[...]
    for r in range(1, ROWS):
        bias = bias + row_of(conv_grad, r)[...]
    small = (bias, gain_acc[...], shift_acc[...], obias_acc[...], scale_acc[...])
    tail = jnp.zeros((CH, COLS), f32)
    for n, x in enumerate(small):
        tail = jnp.where(lane == n, total(x), tail)
    used = jnp.logical_and(lax.rem(lane, 64) >= 28, lax.rem(lane, 64) < 35)
    for p in range(4):
        moved = jnp.where(used, taps_acc[p], 0.0)
        tail = tail + (pltpu.roll(moved, 7 * p, 1) if p else moved)
    extra = win_acc[CH : CH + 8, :]
    turned = jnp.transpose(
        jnp.concatenate([extra[:, :COLS], extra[:, COLS:], jnp.zeros((112, COLS), f32)], axis=0)
    )
    for n in range(4):
        part = turned[CH * (n % 2) : CH * (n % 2) + CH, :]
        tail = jnp.where(lane == 5 + n, pltpu.roll(part, (5 + n - 8 * (n // 2)) % COLS, 1), tail)
    sums[0:64, :] = win_acc[0:CH, :COLS]
    sums[64:128, :] = win_acc[0:CH, COLS:]
    sums[128:256, :] = 0.5 * jnp.concatenate([wout_acc[0:128, :], wout_acc[128:256, :]], axis=1)
    sums[256:320, :] = tail


def spread_body(
    flags,
    conv_grad,
    south,
    north,
    west,
    east,
    taps,
    turned_taps,
    cot,
    mask,
    state,
    delta,
    *rest,
    first,
):
    state_grad, new_state, shifted, near = rest[-4:]
    near_fill(near, north, south)
    build_shifted(
        shifted,
        lambda base, j: pitched(conv_grad, base, j)[...],
        near,
        west,
        east,
        PART,
        lambda base, j: (0, first + base + j),
    )
    on_top = flags[1] == 1
    spot = lax.rem(iota((ROWS, 512), 1), 64)
    beyond = jnp.logical_and(on_top, jnp.logical_and(spot >= 32, spot < 35))

    def step(base, j):
        k = base + j
        band = jnp.where(beyond, banded(taps, base, j), banded(turned_taps, base, j))
        out = jnp.dot(band.astype(bf16), shifted[k], preferred_element_type=f32)
        ocean = mask[...]
        state_grad[k] = (cot[k].astype(f32) * ocean + out).astype(bf16)
        new = ocean * (state[k].astype(f32) + pitched(delta, base, j)[...])
        new_state[k] = new.astype(bf16)

    by_channel(step, 8, PART)


def spread_part(c, held, flags, conv_grad, south, north, west, east, taps, turned, cot, mask, state, delta):
    tall = pl.BlockSpec((PART * PITCH, COLS), lambda _: (c, 0))
    slab = pl.BlockSpec((3, PART, COLS), lambda _: (0, c, 0))
    side = pl.BlockSpec((1, SPAN, COLS), lambda _: (c * PART // 32, 0, 0))
    band = pl.BlockSpec((PART, 512), lambda _: (c, 0))
    block = pl.BlockSpec((PART, ROWS, COLS), lambda _: (c, 0, 0))
    shape = jax.ShapeDtypeStruct((CH, ROWS, COLS), bf16)
    args = (flags, conv_grad, south, north, west, east, taps, turned, cot, mask, state, delta)
    whole = pl.BlockSpec((ROWS, COLS), lambda _: (0, 0))
    specs = [SM, tall, slab, slab, side, side, band, band, block, whole, block, tall]
    kept = [pl.BlockSpec(memory_space=pl.ANY)] * len(held)
    return pl.pallas_call(
        functools.partial(spread_body, first=c * PART % 32),
        grid=(1,),
        out_shape=(shape, shape),
        in_specs=specs + kept,
        out_specs=(block, block),
        scratch_shapes=[
            pltpu.VMEM((PART, 512, COLS), bf16),
            pltpu.VMEM((PART * NEAR, COLS), f32),
        ],
        input_output_aliases={len(args) + n: n for n in range(len(held))},
        compiler_params=pltpu.CompilerParams(vmem_limit_bytes=16 * 1024 * 1024),
        cost_estimate=pl.CostEstimate(flops=1 << 24, bytes_accessed=3 << 20, transcendentals=0),
        name="spread",
    )(*args, *held)


def unpack_body(
    sums, pick, kernel_grad, w_in_grad, w_out_grad, b_in_grad, channel_grads, *, scale
):
    w_in_grad[:, :COLS] = sums[0:64, :] * scale
    w_in_grad[:, COLS:] = sums[64:128, :] * scale
    packed = jnp.transpose(sums[128:256, :] * scale)
    w_out_grad[:, :COLS] = packed[:CH]
    w_out_grad[:, COLS:] = packed[CH:]
    tail = sums[256:320, :] * scale
    turned = jnp.transpose(jnp.concatenate([tail, tail], axis=0))
    kernel_grad[...] = jnp.dot(
        pick[...], turned, preferred_element_type=f32, precision=lax.Precision.HIGHEST
    )[:, :CH]
    channel_grads[...] = turned[0:5, :CH]
    for n in range(4):
        b_in_grad[:, CH * n : CH * n + CH] = turned[5 + n : 6 + n, :CH]


def tap_tables():
    place = np.zeros((49, 512), np.float32)
    turned = np.zeros((49, 512), np.float32)
    pick = np.zeros((49, COLS), np.float32)
    for a in range(7):
        for b in range(7):
            p, g = divmod(b, 2)
            spot = 128 * p + (64 * g + a - 3) % 128
            place[7 * a + b, spot] = 1.0
            turned[48 - (7 * a + b), spot] = 1.0
            pick[7 * a + b, 28 + 7 * p + a + 64 * g] = 1.0
    return place, turned, pick


def row_pairs(lat_size, lon_size):
    first, second = [], []
    for i in range(lat_size):
        for j in range(lon_size):
            me = i * lon_size + j
            first.append((me, (i ^ 1) * lon_size + j))
            if i == lat_size - 1:
                second.append((me, i * lon_size + lon_size - 1 - j))
            elif i > 0:
                other = i + 1 if i % 2 else i - 1
                second.append((me, other * lon_size + j))
    return first, second


def exchange_rows(flags, top, bottom):
    first, second = row_pairs(lax.axis_size("lat"), lax.axis_size("lon"))
    even = flags[0] == 1
    from_a = lax.ppermute(jnp.where(even, top, bottom), AXES, first)
    from_b = lax.ppermute(jnp.where(even, bottom, top), AXES, second)
    return from_a, from_b


def settle_edges(flags, from_a, from_b, rows):
    slab = jax.ShapeDtypeStruct((3, CH, COLS), f32)
    flat = jax.ShapeDtypeStruct((2, SPAN, COLS), f32)
    return call(
        edges_body,
        (slab, slab, flat, flat),
        (flags, from_a, from_b, rows),
        [pltpu.VMEM((CH * NEAR, COLS), f32)],
        smem_first=True,
        flops=1 << 20,
        nbytes=1 << 21,
        name="edges",
    )


def exchange_columns(to_west, to_east):
    lon_size = lax.axis_size("lon")
    up = [(j, (j + 1) % lon_size) for j in range(lon_size)]
    down = [(k, j) for j, k in up]
    west = lax.ppermute(to_east, "lon", up)
    east = lax.ppermute(to_west, "lon", down)
    return west, east


def core_pairs():
    return [(i, i ^ 1) for i in range(32)]


def chip_pairs(flip_x, flip_y, flip_z):
    pairs = []
    for i in range(256):
        lat, lon = divmod(i, 32)
        x = ((lat >> 2) * 2 + (lon >> 4)) ^ flip_x
        y = (lat & 3) ^ flip_y
        z = ((lon >> 1) & 7) ^ flip_z
        pairs.append((i, ((x >> 1) * 4 + y) * 32 + (x & 1) * 16 + z * 2 + (lon & 1)))
    return pairs


def tie(*values):
    return lax.optimization_barrier(values)


def reduce_and_spread(sums, flags, conv_grad, top, bottom, finish):
    odd = lax.rem(lax.axis_index("lon"), 2) == 1
    half = sums.shape[0] // 2
    low, high = sums[:half], sums[half:]
    mine = jnp.where(odd, high, low) + lax.ppermute(jnp.where(odd, low, high), "lon", core_pairs())
    mine, top, bottom = tie(mine, top, bottom)
    from_a, from_b = exchange_rows(flags, top, bottom)

    def hop(x, *flips):
        return x + lax.ppermute(x, AXES, chip_pairs(*flips))

    mine = hop(mine, 1, 0, 0)
    mine, from_a, from_b = tie(hop(mine, 3, 0, 0), from_a, from_b)
    north, south, to_west, to_east = settle_edges(flags, from_a, from_b, conv_grad)
    mine, to_west, to_east = tie(hop(mine, 0, 1, 0), to_west, to_east)
    west, east = exchange_columns(to_west, to_east)
    mine, west, east = tie(hop(mine, 0, 3, 0), west, east)
    done = finish(0, (), south, north, west, east)
    mine, *done = tie(hop(mine, 0, 0, 1), *done)
    done = finish(1, done, south, north, west, east)
    mine, *done = tie(hop(mine, 0, 0, 2), *done)
    done = finish(2, done, south, north, west, east)
    done = finish(3, done, south, north, west, east)
    mine, *done = tie(hop(mine, 0, 0, 4), *done)
    other = lax.ppermute(mine, "lon", core_pairs())
    total = jnp.concatenate([jnp.where(odd, other, mine), jnp.where(odd, mine, other)], axis=0)
    return total, done


def per_device(
    sea_state,
    conv_kernel,
    conv_bias,
    norm_gain,
    norm_shift,
    w_in,
    b_in,
    w_out,
    b_out,
    layer_scale,
    sea_mask,
    cotangent,
):
    lat_size, lon_size = lax.axis_size("lat"), lax.axis_size("lon")
    lat = lax.axis_index("lat")
    flags = jnp.stack([(lat % 2 == 0).astype(jnp.int32), (lat == lat_size - 1).astype(jnp.int32)])
    top = jnp.transpose(sea_state[:, ROWS - 3 :, :].astype(f32), (1, 0, 2))
    bottom = jnp.transpose(sea_state[:, :3, :].astype(f32), (1, 0, 2))
    from_a, from_b = exchange_rows(flags, top, bottom)
    mask = sea_mask.astype(f32)
    place, turned, pick = (jnp.asarray(x) for x in tap_tables())
    taps = jnp.dot(conv_kernel, place.astype(bf16), preferred_element_type=f32)
    turned_taps = jnp.dot(conv_kernel, turned.astype(bf16), preferred_element_type=f32)
    chan = jnp.stack([conv_bias, norm_gain, norm_shift, b_out, layer_scale]).astype(f32)
    chan = jnp.broadcast_to(chan[:, :, None], (5, CH, COLS))
    w_in_t = jnp.concatenate([w_in.T, b_in[:, None], jnp.zeros((HID, 15), bf16)], axis=1)
    half_out = (w_out.astype(f32) * 0.5).astype(bf16)
    north, south, to_west, to_east = settle_edges(flags, from_a, from_b, sea_state)
    halo = (south, north) + exchange_columns(to_west, to_east)
    shifted = pltpu.VMEM((CH, 512, COLS), bf16)
    near = pltpu.VMEM((CH * NEAR, COLS), f32)
    flat = pltpu.VMEM((CH, COLS), f32)
    tall_shape = (CH * PITCH, COLS)
    tall = pltpu.VMEM(tall_shape, f32)
    slab = jax.ShapeDtypeStruct((3, CH, COLS), f32)
    delta, conv_grad, top, bottom, sums = call(
        main_body,
        (
            jax.ShapeDtypeStruct(tall_shape, f32),
            jax.ShapeDtypeStruct(tall_shape, f32),
            slab,
            slab,
            jax.ShapeDtypeStruct((320, COLS), f32),
        ),
        (sea_state,)
        + halo
        + (cotangent, mask, taps, chan, w_in, w_in_t, half_out, half_out.T),
        [
            shifted,
            near,
            tall,
            tall,
            tall,
            pltpu.VMEM((CH + 16, HID), f32),
            pltpu.VMEM((HID, CH), f32),
            flat,
            flat,
            flat,
            flat,
            pltpu.VMEM((4, CH, COLS), f32),
        ],
        flops=1 << 30,
        nbytes=8 << 20,
        name="main",
        mib=28,
    )

    def finish(c, held, *halo):
        rest = (taps, turned_taps, cotangent, mask, sea_state, delta)
        return spread_part(c, held, flags, conv_grad, *halo, *rest)

    total, (state_grad, new_state) = reduce_and_spread(
        sums, flags, conv_grad, top, bottom, finish
    )
    grad_scale = 1.0 / math.sqrt(ROWS * lat_size * COLS * lon_size)
    kernel_grad, w_in_grad, w_out_grad, b_in_grad, channel_grads = call(
        functools.partial(unpack_body, scale=grad_scale),
        (
            jax.ShapeDtypeStruct((49, CH), f32),
            jax.ShapeDtypeStruct((CH, HID), f32),
            jax.ShapeDtypeStruct((CH, HID), f32),
            jax.ShapeDtypeStruct((1, HID), f32),
            jax.ShapeDtypeStruct((5, CH), f32),
        ),
        (total, pick),
        flops=1 << 17,
        nbytes=1 << 18,
        name="unpack",
    )
    return (
        new_state,
        state_grad,
        kernel_grad.T,
        w_in_grad,
        w_out_grad.T,
        b_in_grad.reshape(HID),
        channel_grads,
    )


def solution(mesh):
    grid = P(None, "lat", "lon")
    placed = (grid,) + (P(),) * 9 + (P("lat", "lon"), grid)
    return jax.shard_map(
        per_device,
        mesh=mesh,
        in_specs=placed,
        out_specs=(grid, grid, P(), P(), P(), P(), P()),
        check_vma=False,
    )
```

```python
import functools
import math

import jax
import jax.numpy as jnp
import numpy as np
from jax import lax
from jax.experimental import pallas as pl
from jax.experimental.pallas import tpu as pltpu
from jax.sharding import PartitionSpec as P

slope_coef = 0.044715
tanh_scale = math.sqrt(2.0 / math.pi)
ln_epsilon = 1e-06
f32, bf16 = jnp.float32, jnp.bfloat16

CH, ROWS, COLS, HID = 64, 32, 128, 256
AXES = ("lat", "lon")
VM = pl.BlockSpec(memory_space=pltpu.VMEM)
SM = pl.BlockSpec(memory_space=pltpu.SMEM)
PITCH = ROWS + 1
SPAN = 40
NEAR = 9
PART = 16
TOGETHER = 8


def call(body, out_shape, args, scratch=(), smem_first=False, flops=0, nbytes=0, name=None, mib=8):
    specs = [VM] * len(args)
    if smem_first:
        specs[0] = SM
    return pl.pallas_call(
        body,
        out_shape=out_shape,
        in_specs=specs,
        out_specs=jax.tree.map(lambda _: VM, out_shape),
        scratch_shapes=list(scratch),
        compiler_params=pltpu.CompilerParams(vmem_limit_bytes=mib * 1024 * 1024),
        cost_estimate=pl.CostEstimate(flops=flops, bytes_accessed=nbytes, transcendentals=0),
        name=name,
    )(*args)


def iota(shape, dim):
    return lax.broadcasted_iota(jnp.int32, shape, dim)


def by_channel(step, group=8, count=CH):
    def run(i, carry):
        for j in range(group):
            step(i * group, j)
        return carry

    lax.fori_loop(0, count // group, run, 0)


def pitched(ref, base, j):
    return ref.at[pl.ds(pl.multiple_of(base * PITCH, 8) + j * PITCH, ROWS), :]


def row_of(ref, r):
    return ref.at[pl.ds(r, CH, stride=PITCH), :]


def near_fill(near, north, south):
    near[...] = jnp.zeros_like(near)
    count = north.shape[1]
    for g in range(3):
        near[pl.ds(g, count, stride=NEAR), :] = north[g]
        near[pl.ds(5 + g, count, stride=NEAR), :] = south[g]


def edges_body(flags, from_a, from_b, own, north, south, to_west, to_east, near):
    even = flags[0] == 1
    on_top = flags[1] == 1
    for g in range(3):
        south[g] = jnp.where(even, from_b[g], from_a[g])

    @pl.when(jnp.logical_not(on_top))
    def _():
        for g in range(3):
            north[g] = jnp.where(even, from_a[g], from_b[g])

    @pl.when(on_top)
    def _():
        back = COLS - 1 - iota((CH, COLS), 1)
        for g in range(3):
            got = jnp.where(even, from_a[2 - g], from_b[2 - g])
            north[g] = jnp.take_along_axis(got, back, axis=1)

    near_fill(near, north, south)
    lane = iota((SPAN, COLS), 1)
    for t in range(2):
        west = jnp.zeros((SPAN, COLS), f32)
        east = jnp.zeros((SPAN, COLS), f32)
        for m in range(32):
            k = 32 * t + m
            mine = own[k * PITCH : k * PITCH + ROWS, :] if len(own.shape) == 2 else own[k].astype(f32)
            value = jnp.concatenate([mine, near[k * NEAR : k * NEAR + 8, :]], axis=0)
            here = jnp.logical_and(lane >= 3 * m, lane < 3 * m + 3)
            west = jnp.where(here, pltpu.roll(value, 3 * m, 1) if m else value, west)
            east = jnp.where(here, pltpu.roll(value, 3 * m + 3, 1), east)
        to_west[t] = west
        to_east[t] = east


def build_shifted(shifted, own, near, west, east, count, find):
    lane = iota((SPAN, COLS), 1)
    blank = jnp.zeros((8, COLS), f32)

    def step(base, j):
        k = base + j
        value = jnp.concatenate([own(base, j), near[pl.ds(base * NEAR + j * NEAR, 8), :]], axis=0)
        t, m = find(base, j)
        from_west = pltpu.roll(west[t], 125 - 3 * m, 1)
        from_east = pltpu.roll(east[t], lax.rem(COLS - 3 * m, COLS), 1)
        for b in range(7):
            off = b - 3
            if off == 0:
                v = value
            elif off < 0:
                v = pltpu.roll(jnp.where(lane >= COLS + off, from_west, value), -off, 1)
            else:
                v = pltpu.roll(jnp.where(lane < off, from_east, value), COLS - off, 1)
            p, g = divmod(b, 2)
            mine, other = 128 * p + 64 * g, 128 * p + 64 * (1 - g)
            edge = v[ROWS:]
            shifted[k, mine : mine + 32, :] = v[:ROWS].astype(bf16)
            shifted[k, mine + 32 : mine + 48, :] = jnp.concatenate([edge, blank], 0).astype(bf16)
            shifted[k, other + 48 : other + 64, :] = jnp.concatenate([blank, edge], 0).astype(bf16)
        zero = jnp.zeros((16, COLS), bf16)
        for spot in (384 + 48, 384 + 64, 384 + 80, 384 + 96):
            shifted[k, spot : spot + 16, :] = zero

    by_channel(step, 4, count)


def banded(taps, base, j):
    rows = taps[pl.ds(pl.multiple_of(base, 8), 8), :]
    tiles = []
    for p in range(4):
        row = jnp.broadcast_to(rows[j : j + 1, 128 * p : 128 * p + 128], (8, COLS))
        parts = [pltpu.roll(row, 8 * i, 1, stride=1, stride_axis=0) for i in range(4)]
        tiles.append(jnp.concatenate(parts, axis=0))
    return jnp.concatenate(tiles, axis=1)


def main_body(
    state,
    south,
    north,
    west,
    east,
    cot,
    mask,
    taps,
    chan,
    w_in,
    w_in_t,
    w_out,
    w_out_t,
    delta,
    conv_grad,
    top,
    bottom,
    sums,
    shifted,
    near,
    conv_out,
    cot_rows,
    grad_back,
    win_acc,
    wout_acc,
    gain_acc,
    shift_acc,
    obias_acc,
    scale_acc,
    taps_acc,
):
    near_fill(near, north, south)
    build_shifted(
        shifted,
        lambda base, j: state[base + j].astype(f32),
        near,
        west,
        east,
        CH,
        lambda base, j: (base // 32, lax.rem(base, 32) + j),
    )

    def conv_step(base, j):
        k = base + j
        out = jnp.dot(banded(taps, base, j).astype(bf16), shifted[k], preferred_element_type=f32)
        pitched(conv_out, base, j)[...] = out
        pitched(cot_rows, base, j)[...] = cot[k].astype(f32) * mask[...]

    by_channel(conv_step)

    for acc in (win_acc, wout_acc, gain_acc, shift_acc, obias_acc, scale_acc):
        acc[...] = jnp.zeros_like(acc)

    def wide(x):
        return jnp.concatenate([x] * TOGETHER, axis=1)

    def fold(x):
        return sum(x[:, n * COLS : (n + 1) * COLS] for n in range(TOGETHER))

    def pair(ref, r):
        return jnp.concatenate([row_of(ref, r + n)[...] for n in range(TOGETHER)], axis=1)

    def mean(x):
        return jnp.sum(x, axis=0, keepdims=True) * (1.0 / CH)

    cells = (((1,), (1,)), ((), ()))
    ones = jnp.where(iota((16, TOGETHER * COLS), 0) == 0, 1.0, 0.0).astype(bf16)

    def point_step(i, carry):
        r = TOGETHER * i
        conv_bias, gain, shift, out_bias, scale = (wide(chan[n]) for n in range(5))
        x = pair(conv_out, r) + conv_bias
        centre = x - mean(x)
        inv_std = lax.rsqrt(mean(centre * centre) + ln_epsilon)
        unit = centre * inv_std
        normed = jnp.concatenate([(unit * gain + shift).astype(bf16), ones], axis=0)
        masked_cot = pair(cot_rows, r)
        mixed_grad = (scale * masked_cot).astype(bf16)
        u = jnp.dot(w_in_t[...], normed, preferred_element_type=f32)
        half_grad = jnp.dot(w_out[...], mixed_grad, preferred_element_type=f32)
        bent = (tanh_scale * slope_coef) * (u * u)
        t = jnp.tanh(u * (tanh_scale + bent))
        s = 1.0 + t
        hidden = (u * s).astype(bf16)
        slope = s * (1.0 + (1.0 - t) * (u * (tanh_scale + 3.0 * bent)))
        pre_grad = (half_grad * slope).astype(bf16)
        mixed = jnp.dot(w_out_t[...], hidden, preferred_element_type=f32) + out_bias
        normed_grad = jnp.dot(w_in[...], pre_grad, preferred_element_type=f32)
        win_acc[...] += lax.dot_general(normed, pre_grad, cells, preferred_element_type=f32)
        wout_acc[...] += lax.dot_general(hidden, mixed_grad, cells, preferred_element_type=f32)
        change = scale * mixed
        for n in range(TOGETHER):
            row_of(delta, r + n)[...] = change[:, n * COLS : (n + 1) * COLS]
        scale_acc[...] += fold(masked_cot * mixed)
        obias_acc[...] += fold(mixed_grad.astype(f32))
        slant = normed_grad * unit
        gain_acc[...] += fold(slant)
        shift_acc[...] += fold(normed_grad)
        q = normed_grad * gain
        grad = inv_std * (q - mean(q) - unit * mean(slant * gain))
        for n in range(TOGETHER):
            part = grad[:, n * COLS : (n + 1) * COLS]
            row_of(conv_grad, r + n)[...] = part
            row_of(grad_back, ROWS - 1 - r - n)[...] = part
        return carry

    lax.fori_loop(0, ROWS // TOGETHER, point_step, 0)

    for g in range(3):
        bottom[g] = row_of(conv_grad, g)[...]
        top[g] = row_of(conv_grad, ROWS - 3 + g)[...]

    def grad_step(base, j):
        k = base + j
        back = pitched(grad_back, base, j)[...]
        prod = lax.dot_general(back.astype(bf16), shifted[k], cells, preferred_element_type=f32)
        for p in range(4):
            acc = None
            for i in range(4):
                tile = prod[8 * i : 8 * i + 8, 128 * p : 128 * p + 128]
                tile = pltpu.roll(tile, 8 * i, 1, stride=1, stride_axis=0)
                acc = tile if acc is None else acc + tile
            taps_acc[p, pl.ds(k, 1), :] = jnp.sum(acc, axis=0, keepdims=True)

    by_channel(grad_step, 16)

    lane = iota((CH, COLS), 1)

    def total(x):
        return jnp.broadcast_to(jnp.sum(x, axis=1, keepdims=True), (CH, COLS))

    bias = row_of(conv_grad, 0)[...]
    for r in range(1, ROWS):
        bias = bias + row_of(conv_grad, r)[...]
    small = (bias, gain_acc[...], shift_acc[...], obias_acc[...], scale_acc[...])
    tail = jnp.zeros((CH, COLS), f32)
    for n, x in enumerate(small):
        tail = jnp.where(lane == n, total(x), tail)
    used = jnp.logical_and(lax.rem(lane, 64) >= 28, lax.rem(lane, 64) < 35)
    for p in range(4):
        moved = jnp.where(used, taps_acc[p], 0.0)
        tail = tail + (pltpu.roll(moved, 7 * p, 1) if p else moved)
    extra = win_acc[CH : CH + 8, :]
    turned = jnp.transpose(
        jnp.concatenate([extra[:, :COLS], extra[:, COLS:], jnp.zeros((112, COLS), f32)], axis=0)
    )
    for n in range(4):
        part = turned[CH * (n % 2) : CH * (n % 2) + CH, :]
        tail = jnp.where(lane == 5 + n, pltpu.roll(part, (5 + n - 8 * (n // 2)) % COLS, 1), tail)
    sums[0:64, :] = win_acc[0:CH, :COLS]
    sums[64:128, :] = win_acc[0:CH, COLS:]
    sums[128:256, :] = 0.5 * jnp.concatenate([wout_acc[0:128, :], wout_acc[128:256, :]], axis=1)
    sums[256:320, :] = tail


def spread_body(
    flags,
    conv_grad,
    south,
    north,
    west,
    east,
    taps,
    turned_taps,
    cot,
    mask,
    state,
    delta,
    *rest,
    first,
):
    state_grad, new_state, shifted, near = rest[-4:]
    near_fill(near, north, south)
    build_shifted(
        shifted,
        lambda base, j: pitched(conv_grad, base, j)[...],
        near,
        west,
        east,
        PART,
        lambda base, j: (0, first + base + j),
    )
    on_top = flags[1] == 1
    spot = lax.rem(iota((ROWS, 512), 1), 64)
    beyond = jnp.logical_and(on_top, jnp.logical_and(spot >= 32, spot < 35))

    def step(base, j):
        k = base + j
        band = jnp.where(beyond, banded(taps, base, j), banded(turned_taps, base, j))
        out = jnp.dot(band.astype(bf16), shifted[k], preferred_element_type=f32)
        ocean = mask[...]
        state_grad[k] = (cot[k].astype(f32) * ocean + out).astype(bf16)
        new = ocean * (state[k].astype(f32) + pitched(delta, base, j)[...])
        new_state[k] = new.astype(bf16)

    by_channel(step, 8, PART)


def spread_part(c, held, flags, conv_grad, south, north, west, east, taps, turned, cot, mask, state, delta):
    tall = pl.BlockSpec((PART * PITCH, COLS), lambda _: (c, 0))
    slab = pl.BlockSpec((3, PART, COLS), lambda _: (0, c, 0))
    side = pl.BlockSpec((1, SPAN, COLS), lambda _: (c * PART // 32, 0, 0))
    band = pl.BlockSpec((PART, 512), lambda _: (c, 0))
    block = pl.BlockSpec((PART, ROWS, COLS), lambda _: (c, 0, 0))
    shape = jax.ShapeDtypeStruct((CH, ROWS, COLS), bf16)
    args = (flags, conv_grad, south, north, west, east, taps, turned, cot, mask, state, delta)
    whole = pl.BlockSpec((ROWS, COLS), lambda _: (0, 0))
    specs = [SM, tall, slab, slab, side, side, band, band, block, whole, block, tall]
    kept = [pl.BlockSpec(memory_space=pl.ANY)] * len(held)
    return pl.pallas_call(
        functools.partial(spread_body, first=c * PART % 32),
        grid=(1,),
        out_shape=(shape, shape),
        in_specs=specs + kept,
        out_specs=(block, block),
        scratch_shapes=[
            pltpu.VMEM((PART, 512, COLS), bf16),
            pltpu.VMEM((PART * NEAR, COLS), f32),
        ],
        input_output_aliases={len(args) + n: n for n in range(len(held))},
        compiler_params=pltpu.CompilerParams(vmem_limit_bytes=16 * 1024 * 1024),
        cost_estimate=pl.CostEstimate(flops=1 << 24, bytes_accessed=3 << 20, transcendentals=0),
        name="spread",
    )(*args, *held)


def unpack_body(
    sums, pick, kernel_grad, w_in_grad, w_out_grad, b_in_grad, channel_grads, *, scale
):
    w_in_grad[:, :COLS] = sums[0:64, :] * scale
    w_in_grad[:, COLS:] = sums[64:128, :] * scale
    packed = jnp.transpose(sums[128:256, :] * scale)
    w_out_grad[:, :COLS] = packed[:CH]
    w_out_grad[:, COLS:] = packed[CH:]
    tail = sums[256:320, :] * scale
    turned = jnp.transpose(jnp.concatenate([tail, tail], axis=0))
    kernel_grad[...] = jnp.dot(
        pick[...], turned, preferred_element_type=f32, precision=lax.Precision.HIGHEST
    )[:, :CH]
    channel_grads[...] = turned[0:5, :CH]
    for n in range(4):
        b_in_grad[:, CH * n : CH * n + CH] = turned[5 + n : 6 + n, :CH]


def tap_tables():
    place = np.zeros((49, 512), np.float32)
    turned = np.zeros((49, 512), np.float32)
    pick = np.zeros((49, COLS), np.float32)
    for a in range(7):
        for b in range(7):
            p, g = divmod(b, 2)
            spot = 128 * p + (64 * g + a - 3) % 128
            place[7 * a + b, spot] = 1.0
            turned[48 - (7 * a + b), spot] = 1.0
            pick[7 * a + b, 28 + 7 * p + a + 64 * g] = 1.0
    return place, turned, pick


def row_pairs(lat_size, lon_size):
    first, second = [], []
    for i in range(lat_size):
        for j in range(lon_size):
            me = i * lon_size + j
            first.append((me, (i ^ 1) * lon_size + j))
            if i == lat_size - 1:
                second.append((me, i * lon_size + lon_size - 1 - j))
            elif i > 0:
                other = i + 1 if i % 2 else i - 1
                second.append((me, other * lon_size + j))
    return first, second


def exchange_rows(flags, top, bottom):
    first, second = row_pairs(lax.axis_size("lat"), lax.axis_size("lon"))
    even = flags[0] == 1
    from_a = lax.ppermute(jnp.where(even, top, bottom), AXES, first)
    from_b = lax.ppermute(jnp.where(even, bottom, top), AXES, second)
    return from_a, from_b


def settle_edges(flags, from_a, from_b, rows):
    slab = jax.ShapeDtypeStruct((3, CH, COLS), f32)
    flat = jax.ShapeDtypeStruct((2, SPAN, COLS), f32)
    return call(
        edges_body,
        (slab, slab, flat, flat),
        (flags, from_a, from_b, rows),
        [pltpu.VMEM((CH * NEAR, COLS), f32)],
        smem_first=True,
        flops=1 << 20,
        nbytes=1 << 21,
        name="edges",
    )


def exchange_columns(to_west, to_east):
    lon_size = lax.axis_size("lon")
    up = [(j, (j + 1) % lon_size) for j in range(lon_size)]
    down = [(k, j) for j, k in up]
    west = lax.ppermute(to_east, "lon", up)
    east = lax.ppermute(to_west, "lon", down)
    return west, east


def core_pairs():
    return [(i, i ^ 1) for i in range(32)]


def chip_pairs(flip_x, flip_y, flip_z):
    pairs = []
    for i in range(256):
        lat, lon = divmod(i, 32)
        x = ((lat >> 2) * 2 + (lon >> 4)) ^ flip_x
        y = (lat & 3) ^ flip_y
        z = ((lon >> 1) & 7) ^ flip_z
        pairs.append((i, ((x >> 1) * 4 + y) * 32 + (x & 1) * 16 + z * 2 + (lon & 1)))
    return pairs


def tie(*values):
    return lax.optimization_barrier(values)


def reduce_and_spread(sums, flags, conv_grad, top, bottom, finish):
    odd = lax.rem(lax.axis_index("lon"), 2) == 1
    half = sums.shape[0] // 2
    low, high = sums[:half], sums[half:]
    mine = jnp.where(odd, high, low) + lax.ppermute(jnp.where(odd, low, high), "lon", core_pairs())
    mine, top, bottom = tie(mine, top, bottom)
    from_a, from_b = exchange_rows(flags, top, bottom)

    def hop(x, *flips):
        return x + lax.ppermute(x, AXES, chip_pairs(*flips))

    mine = hop(mine, 0, 1, 0)
    mine, from_a, from_b = tie(hop(mine, 0, 3, 0), from_a, from_b)
    north, south, to_west, to_east = settle_edges(flags, from_a, from_b, conv_grad)
    mine, to_west, to_east = tie(hop(mine, 0, 0, 4), to_west, to_east)
    west, east = exchange_columns(to_west, to_east)
    mine, west, east = tie(hop(mine, 0, 0, 2), west, east)
    done = finish(0, (), south, north, west, east)
    mine, *done = tie(hop(mine, 1, 0, 0), *done)
    done = finish(1, done, south, north, west, east)
    mine, *done = tie(hop(mine, 3, 0, 0), *done)
    done = finish(2, done, south, north, west, east)
    done = finish(3, done, south, north, west, east)
    mine, *done = tie(hop(mine, 0, 0, 1), *done)
    other = lax.ppermute(mine, "lon", core_pairs())
    total = jnp.concatenate([jnp.where(odd, other, mine), jnp.where(odd, mine, other)], axis=0)
    return total, done


def per_device(
    sea_state,
    conv_kernel,
    conv_bias,
    norm_gain,
    norm_shift,
    w_in,
    b_in,
    w_out,
    b_out,
    layer_scale,
    sea_mask,
    cotangent,
):
    lat_size, lon_size = lax.axis_size("lat"), lax.axis_size("lon")
    lat = lax.axis_index("lat")
    flags = jnp.stack([(lat % 2 == 0).astype(jnp.int32), (lat == lat_size - 1).astype(jnp.int32)])
    top = jnp.transpose(sea_state[:, ROWS - 3 :, :].astype(f32), (1, 0, 2))
    bottom = jnp.transpose(sea_state[:, :3, :].astype(f32), (1, 0, 2))
    from_a, from_b = exchange_rows(flags, top, bottom)
    mask = sea_mask.astype(f32)
    place, turned, pick = (jnp.asarray(x) for x in tap_tables())
    taps = jnp.dot(conv_kernel, place.astype(bf16), preferred_element_type=f32)
    turned_taps = jnp.dot(conv_kernel, turned.astype(bf16), preferred_element_type=f32)
    chan = jnp.stack([conv_bias, norm_gain, norm_shift, b_out, layer_scale]).astype(f32)
    chan = jnp.broadcast_to(chan[:, :, None], (5, CH, COLS))
    w_in_t = jnp.concatenate([w_in.T, b_in[:, None], jnp.zeros((HID, 15), bf16)], axis=1)
    half_out = (w_out.astype(f32) * 0.5).astype(bf16)
    north, south, to_west, to_east = settle_edges(flags, from_a, from_b, sea_state)
    halo = (south, north) + exchange_columns(to_west, to_east)
    shifted = pltpu.VMEM((CH, 512, COLS), bf16)
    near = pltpu.VMEM((CH * NEAR, COLS), f32)
    flat = pltpu.VMEM((CH, COLS), f32)
    tall_shape = (CH * PITCH, COLS)
    tall = pltpu.VMEM(tall_shape, f32)
    slab = jax.ShapeDtypeStruct((3, CH, COLS), f32)
    delta, conv_grad, top, bottom, sums = call(
        main_body,
        (
            jax.ShapeDtypeStruct(tall_shape, f32),
            jax.ShapeDtypeStruct(tall_shape, f32),
            slab,
            slab,
            jax.ShapeDtypeStruct((320, COLS), f32),
        ),
        (sea_state,)
        + halo
        + (cotangent, mask, taps, chan, w_in, w_in_t, half_out, half_out.T),
        [
            shifted,
            near,
            tall,
            tall,
            tall,
            pltpu.VMEM((CH + 16, HID), f32),
            pltpu.VMEM((HID, CH), f32),
            flat,
            flat,
            flat,
            flat,
            pltpu.VMEM((4, CH, COLS), f32),
        ],
        flops=1 << 30,
        nbytes=8 << 20,
        name="main",
        mib=28,
    )

    def finish(c, held, *halo):
        rest = (taps, turned_taps, cotangent, mask, sea_state, delta)
        return spread_part(c, held, flags, conv_grad, *halo, *rest)

    total, (state_grad, new_state) = reduce_and_spread(
        sums, flags, conv_grad, top, bottom, finish
    )
    grad_scale = 1.0 / math.sqrt(ROWS * lat_size * COLS * lon_size)
    kernel_grad, w_in_grad, w_out_grad, b_in_grad, channel_grads = call(
        functools.partial(unpack_body, scale=grad_scale),
        (
            jax.ShapeDtypeStruct((49, CH), f32),
            jax.ShapeDtypeStruct((CH, HID), f32),
            jax.ShapeDtypeStruct((CH, HID), f32),
            jax.ShapeDtypeStruct((1, HID), f32),
            jax.ShapeDtypeStruct((5, CH), f32),
        ),
        (total, pick),
        flops=1 << 17,
        nbytes=1 << 18,
        name="unpack",
    )
    return (
        new_state,
        state_grad,
        kernel_grad.T,
        w_in_grad,
        w_out_grad.T,
        b_in_grad.reshape(HID),
        channel_grads,
    )


def solution(mesh):
    grid = P(None, "lat", "lon")
    placed = (grid,) + (P(),) * 9 + (P("lat", "lon"), grid)
    return jax.shard_map(
        per_device,
        mesh=mesh,
        in_specs=placed,
        out_specs=(grid, grid, P(), P(), P(), P(), P()),
        check_vma=False,
    )
```
